512 devices in a mesh: row: 128 (over y, z, core), col: 4 (over x).
Axes of the slice: x: 4, y: 8, z: 8, core: 2. Of those that a mesh axis runs over, the one named last changes fastest.
Arguments:
- tokens: bfloat16 [384, 8192], P('row', 'col'), may hold values from -6 to 6
- gate_weight: float32 [24576, 8192], P('row', 'col'), may hold values from -1 to 1
- up_weight: float32 [24576, 8192], P('row', 'col'), may hold values from -1 to 1
- down_weight: float32 [24576, 8192], P('row', 'col'), may hold values from -1 to 1
- u_init: float32 [3, 24576], P(None, 'row'), may hold values from -6 to 6
- gammas: float32 [3], replicated, may hold values from 2 to 6
Outputs:
- mixed: bfloat16 [384, 8192], P('row', 'col')
- u_out: float32 [3, 24576], P(None, 'row')
- v_out: float32 [3, 8192], P(None, 'col')
The draws below stay inside these ranges and needn't reach their ends.
All inputs are finite; a program needn't handle non-finite values.
Results may differ from the reference program's by a relative error of at most 0.007.
Values may be sent and summed in bfloat16 or wider, within the bound.
A program may use at most 64 MiB of HBM per device.

```python
import math
import jax
import jax.numpy as jnp
from jax import lax

D = 8192
FF = 24576
ITERS = 2
TOKENS = 384


def scaled_matrix(key, rows, cols):
    first, second, third = jax.random.split(key, 3)
    base = jnp.clip(jax.random.normal(first, (rows, cols), jnp.float32), -6.0, 6.0)
    spread = math.log(10.0)
    row_rise = jnp.exp(jnp.arange(rows, dtype=jnp.float32) / rows * math.log(3.0))
    col_rise = jnp.exp(jnp.arange(cols, dtype=jnp.float32) / cols * math.log(3.0))
    row_scale = jnp.exp(jax.random.uniform(second, (rows,), jnp.float32, 0.0, spread)) * row_rise
    col_scale = jnp.exp(jax.random.uniform(third, (cols,), jnp.float32, 0.0, spread)) * col_rise
    values = base * row_scale[:, None] * col_scale[None, :] / (100.0 * math.sqrt(cols))
    return jnp.clip(values, -1.0, 1.0)


def draw_gate_weight(key, part):
    return scaled_matrix(jax.random.fold_in(key, 11), FF, D)


def draw_up_weight(key, part):
    return scaled_matrix(jax.random.fold_in(key, 23), FF, D)


def draw_down_weight(key, part):
    return scaled_matrix(jax.random.fold_in(key, 37), FF, D)


def level_of(key, shape, shards, least, largest):
    def one(position, parts):
        heights = jax.random.uniform(jax.random.fold_in(jax.random.fold_in(key, 6), position), (parts,), jnp.float32, least / len(shards), largest / len(shards))
        return jnp.repeat(jnp.exp(heights), shape[position] // parts).reshape((-1,) + (1,) * (len(shape) - position - 1))

    gain = one(*shards[0])
    for cut in shards[1:]:
        gain = gain * one(*cut)
    return gain


def centred(stream_key, shape, deviation, bound, shards=(), held_as=jnp.bfloat16):
    gain = level_of(stream_key, shape, shards, -0.22, 0.18) if shards else 1.0
    result = jax.random.normal(stream_key, shape, jnp.float32) * deviation * gain
    return jnp.minimum(jnp.maximum(result, -bound), bound).astype(held_as)


def setup_inputs(seed: int = 0) -> dict:
    splits = jax.random.split(jax.random.key(seed), 7)
    return {
        "tokens": centred(splits[0], (TOKENS, D), 1.0, 6.0, ((0, 128), (1, 4))),
        "gate_weight": draw_gate_weight(jax.random.fold_in(splits[6], 71), 0),
        "up_weight": draw_up_weight(jax.random.fold_in(splits[6], 71), 0),
        "down_weight": draw_down_weight(jax.random.fold_in(splits[6], 71), 0),
        "u_init": centred(splits[4], (3, FF), 1.0, 6.0, ((1, 128),), jnp.float32),
        "gammas": jnp.clip(jnp.exp(jax.random.uniform(splits[5], (3,), jnp.float32, math.log(2.0), math.log(6.0))), 2.0, 6.0),
    }


epsilon = 1e-06
highest = lax.Precision.HIGHEST

def power_steps(matrix, start):
    left = start
    right = None
    forward = None
    for step in range(ITERS):
        backward = jnp.dot(left, matrix, precision=highest)
        right = backward / jnp.sqrt(jnp.sum(backward * backward) / D + epsilon)
        forward = jnp.dot(matrix, right, precision=highest)
        left = forward / jnp.sqrt(jnp.sum(forward * forward) / FF + epsilon)
    sigma = jnp.sum(left * forward) / math.sqrt(FF * D)
    return (left, right, sigma)

def reference(tokens, gate_weight, up_weight, down_weight, u_init, gammas):
    matrices = (gate_weight, up_weight, down_weight)
    results = [power_steps(matrices[index], u_init[index]) for index in range(3)]
    scales = [gammas[index] / results[index][2] for index in range(3)]
    gate = jnp.dot(tokens, gate_weight.astype(jnp.bfloat16).T, preferred_element_type=jnp.float32) * scales[0]
    upper = jnp.dot(tokens, up_weight.astype(jnp.bfloat16).T, preferred_element_type=jnp.float32) * scales[1]
    hidden = (jax.nn.silu(gate) * upper).astype(jnp.bfloat16)
    summed = jnp.dot(hidden, down_weight.astype(jnp.bfloat16), preferred_element_type=jnp.float32)
    mixed = (summed * scales[2]).astype(jnp.bfloat16)
    u_out = jnp.stack([results[index][0] for index in range(3)])
    v_out = jnp.stack([results[index][1] for index in range(3)])
    return (mixed, u_out, v_out)
```

```python
import functools
import math

import jax
import jax.numpy as jnp
from jax import lax
from jax.experimental import pallas as pl
from jax.experimental.pallas import tpu as pltpu
from jax.sharding import PartitionSpec as P

MESH = pl.DeviceIdType.MESH
EPS = 1e-06
F32 = jnp.float32
BF16 = jnp.bfloat16


def kernel(
    dims,
    tok_h, wg_h, wu_h, wd_h, ui_h, gam,
    mixed, uout, vout,
    w, w16, d16, ui, tz, tzf, xg, xf,
    part, r1b, r1s, r2b, r2s, bv, bn,
    pk, cb, s3, r3b, s4, r4b,
    gp, xr, ga, hid, rsrc, rdst, acc, qsrc, qdst,
    wsem, lsem, p1s, p1r, p2s, p2r, p3s, p3r, cs, cr,
    e1s, e1r, e2s, e2r, ks, kr, zs, zr, ys, yr,
    gs, gr, hs, hr, fs, fr, qs, qr,
):
    NX, NY, NZ, H, D, T, DT, FT = dims
    NP = 2 * NZ
    HB = H // 8
    ZT = NZ * T
    XT = NY * ZT // NX
    row = lax.axis_index("row")
    x = lax.axis_index("col")
    y = row // NP
    q = lax.rem(row, NP)
    z = q // 2
    c = lax.rem(q, 2)

    def remote(src, dst, ssem, rsem, r, cc):
        return pltpu.make_async_remote_copy(
            src_ref=src, dst_ref=dst, send_sem=ssem, recv_sem=rsem,
            device_id={"row": r, "col": cc}, device_id_type=MESH,
        )

    def each(n, fn):
        def body(d, carry):
            fn(d)
            return carry
        lax.fori_loop(1, n, body, 0)

    def plane(d):
        p = lax.rem(q + d, NP)
        return p, y * NP + p

    def along_y(d):
        p = lax.rem(y + d, NY)
        return p, p * NP + q

    def along_z(d):
        p = lax.rem(z + d, NZ)
        return p, y * NP + p * 2 + c

    def along_x(d):
        return lax.rem(x + d, NX)

    def lanes(p, n=128):
        return pl.ds(pl.multiple_of(p * n, n), n)

    loads = [
        pltpu.make_async_copy(ui_h, ui, lsem.at[0]),
        pltpu.make_async_copy(wg_h, w.at[0], wsem.at[0]),
        pltpu.make_async_copy(wu_h, w.at[1], wsem.at[1]),
        pltpu.make_async_copy(wd_h, w.at[2], wsem.at[2]),
        pltpu.make_async_copy(tok_h, tz.at[z], lsem.at[1]),
    ]
    for load in loads:
        load.start()

    barrier = pltpu.get_barrier_semaphore()

    def greet(r, cc):
        pl.semaphore_signal(
            barrier, inc=1, device_id={"row": r, "col": cc}, device_id_type=MESH
        )

    each(NP, lambda d: greet(plane(d)[1], x))
    each(NY, lambda d: greet(along_y(d)[1], x))
    each(NX, lambda d: greet(row, along_x(d)))

    lane = lax.broadcasted_iota(jnp.int32, (8, 128), 1)
    lane1 = lax.broadcasted_iota(jnp.int32, (1, 128), 1)
    hl = lax.broadcasted_iota(jnp.int32, (8, H), 1)
    hs_ = lax.broadcasted_iota(jnp.int32, (8, H), 0)
    diag = hl - hs_

    def spread(values):
        out = jnp.zeros((1, 128), F32)
        for k in range(3):
            out = jnp.where(lane1 == k, values[k], out)
        return out

    def pick(vector, k):
        return vector[:, k : k + 1]

    def back_first():
        def body(k, carry):
            pltpu.make_async_copy(w.at[k], w.at[k], wsem.at[k]).wait()
            left = jnp.broadcast_to(ui[pl.ds(k, 1), :], (8, H))
            total = jnp.zeros((8, D), F32)
            for rb in range(HB):
                col = jnp.sum(jnp.where(diag == 8 * rb, left, 0.0), axis=1, keepdims=True)
                total = total + w[k, 8 * rb : 8 * rb + 8, :] * col
            part[0, pl.ds(k, 1), :] = jnp.sum(total, axis=0, keepdims=True)
            return carry
        lax.fori_loop(0, 3, body, 0)
        part[0, 3:4, :] = jnp.zeros((1, D), F32)

    def back_second(fore, squares):
        def body(k, carry):
            left = pltpu.roll(fore, lax.rem(128 - k * HB, 128), 1)
            total = jnp.zeros((8, D), F32)
            for rb in range(HB):
                total = total + w[k, 8 * rb : 8 * rb + 8, :] * left[:, rb : rb + 1]
            part[1, pl.ds(k, 1), :] = jnp.sum(total, axis=0, keepdims=True)
            return carry
        lax.fori_loop(0, 3, body, 0)
        line = spread(squares)
        for p in range(NP):
            part[1, 3:4, 128 * p : 128 * p + 128] = line

    def fore_packed(source):
        def body(k, packed):
            b = source[pl.ds(k, 1), :]
            b8 = jnp.broadcast_to(b, (8, D))
            mine = jnp.zeros((8, 128), F32)
            for rb in range(HB):
                got = jnp.sum(w[k, 8 * rb : 8 * rb + 8, :] * b8, axis=1, keepdims=True)
                mine = jnp.where(lane == rb, got, mine)
            packed = packed + pltpu.roll(mine, k * HB, 1)
            square = jnp.sum(b * b, axis=1, keepdims=True)
            return jnp.where(lane == 3 * HB + k, square, packed)
        return lax.fori_loop(0, 3, body, jnp.zeros((8, 128), F32))

    def leg1(t):
        return lambda d: remote(
            part.at[t, :, lanes(plane(d)[0])], r1b.at[t, q],
            p1s.at[t, d], p1r.at[t, d], plane(d)[1], x,
        )

    def leg2(t):
        return lambda d: remote(
            r1s.at[t], r2b.at[t, y], p2s.at[t, d], p2r.at[t, d], along_y(d)[1], x
        )

    def leg3(t):
        return lambda d: remote(
            r2s.at[t], bv.at[t, :, lanes(q)], p3s.at[t, d], p3r.at[t, d], plane(d)[1], x
        )

    def start1(t):
        each(NP, lambda d: leg1(t)(d).start())
        r1b[t, q] = part[t, :, lanes(q)]

    def start2(t):
        each(NP, lambda d: leg1(t)(d).wait_recv())
        total = r1b[t, 0]
        for p in range(1, NP):
            total = total + r1b[t, p]
        r1s[t] = total
        each(NY, lambda d: leg2(t)(d).start())
        r2b[t, y] = total

    def start3(t):
        each(NY, lambda d: leg2(t)(d).wait_recv())
        total = r2b[t, 0]
        for p in range(1, NY):
            total = total + r2b[t, p]
        r2s[t] = total
        each(NP, lambda d: leg3(t)(d).start())
        bv[t, :, lanes(q)] = total

    def finish3(t):
        each(NP, lambda d: leg3(t)(d).wait_recv())

    def cross(t):
        return lambda d: remote(
            pk.at[t], cb.at[t, x], cs.at[t, d], cr.at[t, d], row, along_x(d)
        )

    def col_start(t, packed):
        pk[t] = packed
        each(NX, lambda d: cross(t)(d).start())
        cb[t, x] = packed

    def col_finish(t):
        each(NX, lambda d: cross(t)(d).wait_recv())
        total = cb[t, 0]
        for p in range(1, NX):
            total = total + cb[t, p]
        roots = [
            jnp.sqrt(total[0:1, 3 * HB + k : 3 * HB + k + 1] / DT + EPS) for k in range(3)
        ]
        line = jnp.where(lane1 < HB, roots[0], jnp.where(lane1 < 2 * HB, roots[1], roots[2]))
        fore = jnp.where(lane < 3 * HB, total / line, 0.0)
        squares = []
        for k in range(3):
            own = jnp.where((lane >= k * HB) & (lane < (k + 1) * HB), fore * fore, 0.0)
            own = jnp.sum(own, axis=1, keepdims=True)
            squares.append(jnp.sum(own, axis=0, keepdims=True))
        return fore, squares, roots

    swap = [
        remote(w16.at[pl.ds(pl.multiple_of(c * H, H), H)], w16.at[pl.ds(pl.multiple_of(c * H, H), H)],
               ks.at[0], kr.at[0], row + 1 - 2 * c, x),
        remote(w16.at[pl.ds(pl.multiple_of((2 + c) * H, H), H)], w16.at[pl.ds(pl.multiple_of((2 + c) * H, H), H)],
               ks.at[1], kr.at[1], row + 1 - 2 * c, x),
        remote(d16.at[pl.ds(pl.multiple_of(c * H, H), H)], d16.at[pl.ds(pl.multiple_of(c * H, H), H)],
               ks.at[2], kr.at[2], row + 1 - 2 * c, x),
    ]

    def tokens_z(d):
        return remote(tok_h, tz.at[z], zs.at[d], zr.at[d], along_z(d)[1], x)

    def tokens_y(d):
        return remote(xg.at[y], xg.at[y], ys.at[d], yr.at[d], along_y(d)[1], x)

    def gates_out(d):
        return remote(
            gp.at[pl.ds(pl.multiple_of(along_x(d) * XT, XT), XT)], xr.at[x],
            gs.at[d], gr.at[d], row, along_x(d),
        )

    def gates_back(d):
        mine = ga.at[pl.ds(pl.multiple_of(x * XT, XT), XT)]
        return remote(mine, mine, hs.at[d], hr.at[d], row, along_x(d))

    def sums_y(d):
        return remote(rsrc.at[along_y(d)[0]], rdst.at[y], fs.at[d], fr.at[d], along_y(d)[1], x)

    def sums_z(d):
        return remote(qsrc.at[along_z(d)[0]], qdst.at[z], qs.at[d], qr.at[d], along_z(d)[1], x)

    loads[0].wait()
    back_first()
    pl.semaphore_wait(barrier, (NP - 1) + (NY - 1) + (NX - 1))
    start1(0)
    each(NZ, lambda d: tokens_z(d).start())
    w16[pl.ds(pl.multiple_of(c * H, H), H), :] = w[0].astype(BF16)
    swap[0].start()
    w16[pl.ds(pl.multiple_of((2 + c) * H, H), H), :] = w[1].astype(BF16)
    swap[1].start()
    start2(0)

    loads[4].wait()
    each(NZ, lambda d: tokens_z(d).wait_recv())
    for p in range(NZ):
        tzf[T * p : T * p + T, :] = tz[p].astype(F32)
    xg[y] = tzf[...].astype(BF16)
    each(NY, lambda d: tokens_y(d).start())
    start3(0)

    d16[pl.ds(pl.multiple_of(c * H, H), H), :] = w[2].astype(BF16)
    swap[2].start()
    finish3(0)
    col_start(0, fore_packed(bv.at[0]))
    fore, squares, _ = col_finish(0)
    back_second(fore, squares)
    start1(1)

    each(NY, lambda d: tokens_y(d).wait_recv())
    for p in range(NY):
        xf[ZT * p : ZT * p + ZT, :] = xg[p].astype(F32)
    swap[0].wait_recv()
    swap[1].wait_recv()

    width = min(256, 4 * H)

    def gate_block(n, carry):
        gp[:, lanes(n, width)] = lax.dot_general(
            xf[...].astype(BF16), w16[pl.ds(pl.multiple_of(n * width, width), width), :],
            (((1,), (1,)), ((), ())), preferred_element_type=F32,
        )
        return carry

    lax.fori_loop(0, 4 * H // width, gate_block, 0)
    each(NX, lambda d: gates_out(d).start())
    xr[x] = gp[pl.ds(pl.multiple_of(x * XT, XT), XT), :]

    start2(1)
    start3(1)
    each(NX, lambda d: gates_out(d).wait_recv())
    total = xr[0]
    for p in range(1, NX):
        total = total + xr[p]
    ga[pl.ds(pl.multiple_of(x * XT, XT), XT), :] = total
    each(NX, lambda d: gates_back(d).start())
    finish3(1)

    line = bv[1, 3:4, 0:128]
    for k in range(3):
        bn[k : k + 1, :] = bv[1, k : k + 1, :] / jnp.sqrt(pick(line, k) / FT + EPS)
    col_start(1, fore_packed(bn))
    fore, squares, roots = col_finish(1)

    def len1(d):
        return remote(s3, r3b.at[q], e1s.at[d], e1r.at[d], plane(d)[1], x)

    def len2(d):
        return remote(s4, r4b.at[y], e2s.at[d], e2r.at[d], along_y(d)[1], x)

    line = spread(squares)
    s3[...] = line
    each(NP, lambda d: len1(d).start())
    r3b[q] = line
    for k in range(3):
        vout[k : k + 1, :] = bn[k : k + 1, :] / roots[k]
    each(NX, lambda d: gates_back(d).wait_recv())
    each(NP, lambda d: len1(d).wait_recv())
    line = r3b[0]
    for p in range(1, NP):
        line = line + r3b[p]
    s4[...] = line
    each(NY, lambda d: len2(d).start())
    r4b[y] = line
    swap[2].wait_recv()
    each(NY, lambda d: len2(d).wait_recv())
    line = r4b[0]
    for p in range(1, NY):
        line = line + r4b[p]

    lengths = [jnp.sqrt(pick(line, k) / FT + EPS) for k in range(3)]
    sigmas = [pick(line, k) / lengths[k] / math.sqrt(FT * DT) for k in range(3)]
    scales = [gam[k] / sigmas[k] for k in range(3)]

    gate = ga[:, 0 : 2 * H] * scales[0]
    upper = ga[:, 2 * H : 4 * H] * scales[1]
    hid[...] = (gate * jax.nn.sigmoid(gate) * upper).astype(BF16)

    def down_block(n, carry):
        out = jnp.dot(hid[...], d16[:, lanes(n, 256)], preferred_element_type=F32)
        for p in range(NY):
            rsrc[p, :, lanes(n, 256)] = out[ZT * p : ZT * p + ZT].astype(BF16)
        return carry

    lax.fori_loop(0, D // 256, down_block, 0)
    each(NY, lambda d: sums_y(d).start())
    rdst[y] = rsrc[y]

    left = fore / jnp.where(lane1 < HB, lengths[0], jnp.where(lane1 < 2 * HB, lengths[1], lengths[2]))

    def unpack(k, carry):
        own = pltpu.roll(left, lax.rem(128 - k * HB, 128), 1)
        rows = jnp.zeros((8, H), F32)
        for rb in range(HB):
            rows = jnp.where(diag == 8 * rb, own[:, rb : rb + 1], rows)
        keep = (diag >= 0) & (lax.rem(diag, 8) == 0)
        rows = jnp.where(keep, rows, 0.0)
        uout[pl.ds(k, 1), :] = jnp.sum(rows, axis=0, keepdims=True)
        return carry

    lax.fori_loop(0, 3, unpack, 0)

    each(NY, lambda d: sums_y(d).wait_recv())
    total = rdst[0].astype(F32)
    for p in range(1, NY):
        total = total + rdst[p].astype(F32)
    acc[...] = total
    for p in range(NZ):
        qsrc[p] = acc[T * p : T * p + T, :].astype(BF16)
    each(NZ, lambda d: sums_z(d).start())
    qdst[z] = qsrc[z]
    each(NZ, lambda d: sums_z(d).wait_recv())
    total = qdst[0].astype(F32)
    for p in range(1, NZ):
        total = total + qdst[p].astype(F32)
    mixed[...] = (total * scales[2]).astype(BF16)

    for t in range(2):
        each(NP, lambda d: leg1(t)(d).wait_send())
        each(NY, lambda d: leg2(t)(d).wait_send())
        each(NP, lambda d: leg3(t)(d).wait_send())
        each(NX, lambda d: cross(t)(d).wait_send())
    for copy in swap:
        copy.wait_send()
    each(NZ, lambda d: tokens_z(d).wait_send())
    each(NY, lambda d: tokens_y(d).wait_send())
    each(NX, lambda d: gates_out(d).wait_send())
    each(NX, lambda d: gates_back(d).wait_send())
    each(NP, lambda d: len1(d).wait_send())
    each(NY, lambda d: len2(d).wait_send())
    each(NY, lambda d: sums_y(d).wait_send())
    each(NZ, lambda d: sums_z(d).wait_send())


def solution(mesh):
    rows, NX = mesh.shape["row"], mesh.shape["col"]
    NZ = math.isqrt(rows // 2)
    NY = rows // 2 // NZ
    NP = 2 * NZ

    def per_device(tokens, gate_weight, up_weight, down_weight, u_init, gammas):
        T, D = tokens.shape
        H = gate_weight.shape[0]
        ZT = NZ * T
        NT = NY * ZT
        XT = NT // NX
        dims = (NX, NY, NZ, H, D, T, D * NX, H * rows)
        V = pltpu.VMEM
        dma = pltpu.SemaphoreType.DMA
        anywhere = pl.BlockSpec(memory_space=pl.ANY)
        vmem = pl.BlockSpec(memory_space=pltpu.VMEM)
        return pl.pallas_call(
            functools.partial(kernel, dims),
            out_shape=(
                jax.ShapeDtypeStruct((T, D), BF16),
                jax.ShapeDtypeStruct((3, H), F32),
                jax.ShapeDtypeStruct((3, D), F32),
            ),
            in_specs=[anywhere] * 5 + [pl.BlockSpec(memory_space=pltpu.SMEM)],
            out_specs=(vmem, vmem, vmem),
            scratch_shapes=[
                V((3, H, D), F32), V((4 * H, D), BF16), V((2 * H, D), BF16), V((3, H), F32),
                V((NZ, T, D), BF16), V((ZT, D), F32), V((NY, ZT, D), BF16), V((NT, D), F32),
                V((2, 4, D), F32), V((2, NP, 4, 128), F32), V((2, 4, 128), F32),
                V((2, NY, 4, 128), F32), V((2, 4, 128), F32), V((2, 4, D), F32), V((3, D), F32),
                V((2, 8, 128), F32), V((2, NX, 8, 128), F32),
                V((1, 128), F32), V((NP, 1, 128), F32), V((1, 128), F32), V((NY, 1, 128), F32),
                V((NT, 4 * H), F32), V((NX, XT, 4 * H), F32), V((NT, 4 * H), F32), V((NT, 2 * H), BF16),
                V((NY, ZT, D), BF16), V((NY, ZT, D), BF16), V((ZT, D), F32),
                V((NZ, T, D), BF16), V((NZ, T, D), BF16),
                dma((3,)), dma((2,)),
                dma((2, NP)), dma((2, NP)), dma((2, NY)), dma((2, NY)), dma((2, NP)), dma((2, NP)),
                dma((2, NX)), dma((2, NX)),
                dma((NP,)), dma((NP,)), dma((NY,)), dma((NY,)), dma((3,)), dma((3,)),
                dma((NZ,)), dma((NZ,)), dma((NY,)), dma((NY,)),
                dma((NX,)), dma((NX,)), dma((NX,)), dma((NX,)),
                dma((NY,)), dma((NY,)), dma((NZ,)), dma((NZ,)),
            ],
            compiler_params=pltpu.CompilerParams(
                collective_id=0, has_side_effects=True, vmem_limit_bytes=60 * 1024 * 1024
            ),
        )(tokens, gate_weight, up_weight, down_weight, u_init, gammas)

    return jax.shard_map(
        per_device,
        mesh=mesh,
        in_specs=(
            P("row", "col"),
            P("row", "col"),
            P("row", "col"),
            P("row", "col"),
            P(None, "row"),
            P(),
        ),
        out_specs=(P("row", "col"), P(None, "row"), P(None, "col")),
        check_vma=False,
    )
```

```python
import functools
import math

import jax
import jax.numpy as jnp
from jax import lax
from jax.experimental import pallas as pl
from jax.experimental.pallas import tpu as pltpu
from jax.sharding import PartitionSpec as P

MESH = pl.DeviceIdType.MESH
EPS = 1e-06
F32 = jnp.float32
BF16 = jnp.bfloat16


def kernel(
    dims,
    tok_h, wg_h, wu_h, wd_h, ui_h, gam_h,
    mixed, uout, vout,
    gam, w, w16, d16, ui, ta, tb, tzf, xa, xb, xf, x16, perm,
    part, r1b, r1s, r2b, r2s, bv, bn,
    pk, cb, s3, r3b, s4, r4b,
    gp, xr, ga, hid, asrc, adst, bsrc, bdst, acc, aq, ar, bq, br,
    wsem, lsem, p1s, p1r, p2s, p2r, p3s, p3r, cs, cr,
    e1s, e1r, e2s, e2r, ks, kr, ta1s, ta1r, tb1s, tb1r, ta2s, ta2r, tb2s, tb2r,
    gs, gr, hs, hr, as1, ar1, bs1, br1, as2, ar2, bs2, br2,
):
    NX, NY, NZ, H, D, T, DT, FT = dims
    NP = 2 * NZ
    HB = H // 8
    ZT = NZ * T
    YT = NY * T
    XT = NY * ZT // NX
    W = D // 2
    row = lax.axis_index("row")
    x = lax.axis_index("col")
    y = row // NP
    q = lax.rem(row, NP)
    z = q // 2
    c = lax.rem(q, 2)

    def remote(src, dst, ssem, rsem, r, cc):
        return pltpu.make_async_remote_copy(
            src_ref=src, dst_ref=dst, send_sem=ssem, recv_sem=rsem,
            device_id={"row": r, "col": cc}, device_id_type=MESH,
        )

    def each(n, fn):
        def body(d, carry):
            fn(d)
            return carry
        lax.fori_loop(1, n, body, 0)

    def plane(d):
        p = lax.rem(q + d, NP)
        return p, y * NP + p

    def along_y(d):
        p = lax.rem(y + d, NY)
        return p, p * NP + q

    def along_z(d):
        p = lax.rem(z + d, NZ)
        return p, y * NP + p * 2 + c

    def along_x(d):
        return lax.rem(x + d, NX)

    def lanes(p, n=128):
        return pl.ds(pl.multiple_of(p * n, n), n)

    loads = [
        pltpu.make_async_copy(ui_h, ui, lsem.at[0]),
        pltpu.make_async_copy(wg_h, w.at[0], wsem.at[0]),
        pltpu.make_async_copy(wu_h, w.at[1], wsem.at[1]),
        pltpu.make_async_copy(wd_h, w.at[2], wsem.at[2]),
        pltpu.make_async_copy(tok_h.at[:, 0:W], ta.at[z], lsem.at[1]),
        pltpu.make_async_copy(tok_h.at[:, W:D], tb.at[y], lsem.at[2]),
        pltpu.make_async_copy(gam_h, gam, lsem.at[3]),
    ]
    for load in loads:
        load.start()

    barrier = pltpu.get_barrier_semaphore()

    def greet(r, cc):
        pl.semaphore_signal(
            barrier, inc=1, device_id={"row": r, "col": cc}, device_id_type=MESH
        )

    each(NP, lambda d: greet(plane(d)[1], x))
    each(NY, lambda d: greet(along_y(d)[1], x))
    each(NX, lambda d: greet(row, along_x(d)))

    lane = lax.broadcasted_iota(jnp.int32, (8, 128), 1)
    lane1 = lax.broadcasted_iota(jnp.int32, (1, 128), 1)
    hl = lax.broadcasted_iota(jnp.int32, (8, H), 1)
    hs_ = lax.broadcasted_iota(jnp.int32, (8, H), 0)
    diag = hl - hs_

    def spread(values):
        out = jnp.zeros((1, 128), F32)
        for k in range(3):
            out = jnp.where(lane1 == k, values[k], out)
        return out

    def pick(vector, k):
        return vector[:, k : k + 1]

    def back_first():
        def body(k, carry):
            pltpu.make_async_copy(w.at[k], w.at[k], wsem.at[k]).wait()
            left = jnp.broadcast_to(ui[pl.ds(k, 1), :], (8, H))
            total = jnp.zeros((8, D), F32)
            for rb in range(HB):
                col = jnp.sum(jnp.where(diag == 8 * rb, left, 0.0), axis=1, keepdims=True)
                total = total + w[k, 8 * rb : 8 * rb + 8, :] * col
            part[0, pl.ds(k, 1), :] = jnp.sum(total, axis=0, keepdims=True)
            return carry
        lax.fori_loop(0, 3, body, 0)
        part[0, 3:4, :] = jnp.zeros((1, D), F32)

    def back_second(fore, squares):
        def body(k, carry):
            left = pltpu.roll(fore, lax.rem(128 - k * HB, 128), 1)
            total = jnp.zeros((8, D), F32)
            for rb in range(HB):
                total = total + w[k, 8 * rb : 8 * rb + 8, :] * left[:, rb : rb + 1]
            part[1, pl.ds(k, 1), :] = jnp.sum(total, axis=0, keepdims=True)
            return carry
        lax.fori_loop(0, 3, body, 0)
        line = spread(squares)
        for p in range(NP):
            part[1, 3:4, 128 * p : 128 * p + 128] = line

    def fore_packed(source):
        def body(k, packed):
            b = source[pl.ds(k, 1), :]
            b8 = jnp.broadcast_to(b, (8, D))
            mine = jnp.zeros((8, 128), F32)
            for rb in range(HB):
                got = jnp.sum(w[k, 8 * rb : 8 * rb + 8, :] * b8, axis=1, keepdims=True)
                mine = jnp.where(lane == rb, got, mine)
            packed = packed + pltpu.roll(mine, k * HB, 1)
            square = jnp.sum(b * b, axis=1, keepdims=True)
            return jnp.where(lane == 3 * HB + k, square, packed)
        return lax.fori_loop(0, 3, body, jnp.zeros((8, 128), F32))

    def leg1(t):
        return lambda d: remote(
            part.at[t, :, lanes(plane(d)[0])], r1b.at[t, q],
            p1s.at[t, d], p1r.at[t, d], plane(d)[1], x,
        )

    def leg2(t):
        return lambda d: remote(
            r1s.at[t], r2b.at[t, y], p2s.at[t, d], p2r.at[t, d], along_y(d)[1], x
        )

    def leg3(t):
        return lambda d: remote(
            r2s.at[t], bv.at[t, :, lanes(q)], p3s.at[t, d], p3r.at[t, d], plane(d)[1], x
        )

    def start1(t):
        each(NP, lambda d: leg1(t)(d).start())
        r1b[t, q] = part[t, :, lanes(q)]

    def start2(t):
        each(NP, lambda d: leg1(t)(d).wait_recv())
        total = r1b[t, 0]
        for p in range(1, NP):
            total = total + r1b[t, p]
        r1s[t] = total
        each(NY, lambda d: leg2(t)(d).start())
        r2b[t, y] = total

    def start3(t):
        each(NY, lambda d: leg2(t)(d).wait_recv())
        total = r2b[t, 0]
        for p in range(1, NY):
            total = total + r2b[t, p]
        r2s[t] = total
        each(NP, lambda d: leg3(t)(d).start())
        bv[t, :, lanes(q)] = total

    def finish3(t):
        each(NP, lambda d: leg3(t)(d).wait_recv())

    def cross(t):
        return lambda d: remote(
            pk.at[t], cb.at[t, x], cs.at[t, d], cr.at[t, d], row, along_x(d)
        )

    def col_start(t, packed):
        pk[t] = packed
        each(NX, lambda d: cross(t)(d).start())
        cb[t, x] = packed

    def col_finish(t):
        each(NX, lambda d: cross(t)(d).wait_recv())
        total = cb[t, 0]
        for p in range(1, NX):
            total = total + cb[t, p]
        roots = [
            jnp.sqrt(total[0:1, 3 * HB + k : 3 * HB + k + 1] / DT + EPS) for k in range(3)
        ]
        line = jnp.where(lane1 < HB, roots[0], jnp.where(lane1 < 2 * HB, roots[1], roots[2]))
        fore = jnp.where(lane < 3 * HB, total / line, 0.0)
        squares = []
        for k in range(3):
            own = jnp.where((lane >= k * HB) & (lane < (k + 1) * HB), fore * fore, 0.0)
            own = jnp.sum(own, axis=1, keepdims=True)
            squares.append(jnp.sum(own, axis=0, keepdims=True))
        return fore, squares, roots

    swap = [
        remote(w16.at[pl.ds(pl.multiple_of(c * H, H), H)], w16.at[pl.ds(pl.multiple_of(c * H, H), H)],
               ks.at[0], kr.at[0], row + 1 - 2 * c, x),
        remote(w16.at[pl.ds(pl.multiple_of((2 + c) * H, H), H)], w16.at[pl.ds(pl.multiple_of((2 + c) * H, H), H)],
               ks.at[1], kr.at[1], row + 1 - 2 * c, x),
        remote(d16.at[pl.ds(pl.multiple_of(c * H, H), H)], d16.at[pl.ds(pl.multiple_of(c * H, H), H)],
               ks.at[2], kr.at[2], row + 1 - 2 * c, x),
    ]

    def tok_a1(d):
        return remote(tok_h.at[:, 0:W], ta.at[z], ta1s.at[d], ta1r.at[d], along_z(d)[1], x)

    def tok_b1(d):
        return remote(tok_h.at[:, W:D], tb.at[y], tb1s.at[d], tb1r.at[d], along_y(d)[1], x)

    def tok_a2(d):
        return remote(xa.at[y], xa.at[y], ta2s.at[d], ta2r.at[d], along_y(d)[1], x)

    def tok_b2(d):
        return remote(xb.at[z], xb.at[z], tb2s.at[d], tb2r.at[d], along_z(d)[1], x)

    def gates_out(d):
        return remote(
            gp.at[pl.ds(pl.multiple_of(along_x(d) * XT, XT), XT)], xr.at[x],
            gs.at[d], gr.at[d], row, along_x(d),
        )

    def gates_back(d):
        mine = ga.at[pl.ds(pl.multiple_of(x * XT, XT), XT)]
        return remote(mine, mine, hs.at[d], hr.at[d], row, along_x(d))

    def sum_a1(d):
        return remote(asrc.at[along_y(d)[0]], adst.at[y], as1.at[d], ar1.at[d], along_y(d)[1], x)

    def sum_b1(d):
        return remote(bsrc.at[along_z(d)[0]], bdst.at[z], bs1.at[d], br1.at[d], along_z(d)[1], x)

    def sum_a2(d):
        return remote(aq.at[along_z(d)[0]], ar.at[z], as2.at[d], ar2.at[d], along_z(d)[1], x)

    def sum_b2(d):
        return remote(bq.at[along_y(d)[0]], br.at[y], bs2.at[d], br2.at[d], along_y(d)[1], x)

    loads[0].wait()
    back_first()
    pl.semaphore_wait(barrier, (NP - 1) + (NY - 1) + (NX - 1))
    start1(0)
    each(NZ, lambda d: tok_a1(d).start())
    each(NY, lambda d: tok_b1(d).start())
    w16[pl.ds(pl.multiple_of(c * H, H), H), :] = w[0].astype(BF16)
    swap[0].start()
    w16[pl.ds(pl.multiple_of((2 + c) * H, H), H), :] = w[1].astype(BF16)
    swap[1].start()
    d16[pl.ds(pl.multiple_of(c * H, H), H), :] = w[2].astype(BF16)
    swap[2].start()
    start2(0)

    loads[4].wait()
    each(NZ, lambda d: tok_a1(d).wait_recv())
    for p in range(NZ):
        tzf[T * p : T * p + T, :] = ta[p].astype(F32)
    xa[y] = tzf[...].astype(BF16)
    each(NY, lambda d: tok_a2(d).start())
    loads[5].wait()
    each(NY, lambda d: tok_b1(d).wait_recv())
    for p in range(NY):
        tzf[T * p : T * p + T, :] = tb[p].astype(F32)
    xb[z] = tzf[...].astype(BF16)
    lo = lax.broadcasted_iota(jnp.int32, (NY * ZT, NY * ZT), 0)
    hi = lax.broadcasted_iota(jnp.int32, (NY * ZT, NY * ZT), 1)
    major = jnp.zeros_like(lo)
    for p in range(1, NY):
        major = major + (lo >= p * ZT).astype(jnp.int32)
    minor = jnp.zeros_like(lo)
    for p in range(1, NZ):
        minor = minor + (lo - major * ZT >= p * T).astype(jnp.int32)
    wanted = minor * YT + major * T + (lo - major * ZT - minor * T)
    perm[...] = jnp.where(hi == wanted, 1.0, 0.0).astype(BF16)
    start3(0)
    each(NZ, lambda d: tok_b2(d).start())
    finish3(0)
    col_start(0, fore_packed(bv.at[0]))
    fore, squares, _ = col_finish(0)
    back_second(fore, squares)
    start1(1)

    each(NY, lambda d: tok_a2(d).wait_recv())
    for p in range(NY):
        xf[ZT * p : ZT * p + ZT, :] = xa[p].astype(F32)
    x16[:, 0:W] = xf[...].astype(BF16)
    each(NZ, lambda d: tok_b2(d).wait_recv())
    for p in range(NZ):
        xf[YT * p : YT * p + YT, :] = xb[p].astype(F32)
    x16[:, W:D] = jnp.dot(
        perm[...], xf[...].astype(BF16), preferred_element_type=F32
    ).astype(BF16)
    swap[0].wait_recv()
    swap[1].wait_recv()
    gp[...] = lax.dot_general(
        x16[...], w16[...], (((1,), (1,)), ((), ())), preferred_element_type=F32
    )
    each(NX, lambda d: gates_out(d).start())
    xr[x] = gp[pl.ds(pl.multiple_of(x * XT, XT), XT), :]

    start2(1)
    start3(1)
    each(NX, lambda d: gates_out(d).wait_recv())
    total = xr[0]
    for p in range(1, NX):
        total = total + xr[p]
    ga[pl.ds(pl.multiple_of(x * XT, XT), XT), :] = total
    finish3(1)

    line = bv[1, 3:4, 0:128]
    for k in range(3):
        bn[k : k + 1, :] = bv[1, k : k + 1, :] / jnp.sqrt(pick(line, k) / FT + EPS)
    col_start(1, fore_packed(bn))
    each(NX, lambda d: gates_back(d).start())
    fore, squares, roots = col_finish(1)

    def len1(d):
        return remote(s3, r3b.at[q], e1s.at[d], e1r.at[d], plane(d)[1], x)

    def len2(d):
        return remote(s4, r4b.at[y], e2s.at[d], e2r.at[d], along_y(d)[1], x)

    line = spread(squares)
    s3[...] = line
    each(NP, lambda d: len1(d).start())
    r3b[q] = line
    for k in range(3):
        vout[k : k + 1, :] = bn[k : k + 1, :] / roots[k]
    each(NP, lambda d: len1(d).wait_recv())
    line = r3b[0]
    for p in range(1, NP):
        line = line + r3b[p]
    s4[...] = line
    each(NY, lambda d: len2(d).start())
    r4b[y] = line
    swap[2].wait_recv()
    each(NX, lambda d: gates_back(d).wait_recv())
    each(NY, lambda d: len2(d).wait_recv())
    line = r4b[0]
    for p in range(1, NY):
        line = line + r4b[p]

    loads[6].wait()
    lengths = [jnp.sqrt(pick(line, k) / FT + EPS) for k in range(3)]
    sigmas = [pick(line, k) / lengths[k] / math.sqrt(FT * DT) for k in range(3)]
    scales = [gam[k] / sigmas[k] for k in range(3)]

    gate = ga[:, 0 : 2 * H] * scales[0]
    upper = ga[:, 2 * H : 4 * H] * scales[1]
    hid[...] = (gate * jax.nn.sigmoid(gate) * upper).astype(BF16)

    out = jnp.dot(hid[...], d16[:, 0:W], preferred_element_type=F32)
    for p in range(NY):
        asrc[p] = out[ZT * p : ZT * p + ZT].astype(BF16)
    each(NY, lambda d: sum_a1(d).start())
    turned = jnp.dot(perm[...], hid[...], preferred_element_type=F32).astype(BF16)
    out = jnp.dot(turned, d16[:, W:D], preferred_element_type=F32)
    for p in range(NZ):
        bsrc[p] = out[YT * p : YT * p + YT].astype(BF16)
    each(NZ, lambda d: sum_b1(d).start())
    adst[y] = asrc[y]
    bdst[z] = bsrc[z]

    left = fore / jnp.where(lane1 < HB, lengths[0], jnp.where(lane1 < 2 * HB, lengths[1], lengths[2]))

    def unpack(k, carry):
        own = pltpu.roll(left, lax.rem(128 - k * HB, 128), 1)
        rows = jnp.zeros((8, H), F32)
        for rb in range(HB):
            rows = jnp.where(diag == 8 * rb, own[:, rb : rb + 1], rows)
        keep = (diag >= 0) & (lax.rem(diag, 8) == 0)
        rows = jnp.where(keep, rows, 0.0)
        uout[pl.ds(k, 1), :] = jnp.sum(rows, axis=0, keepdims=True)
        return carry

    lax.fori_loop(0, 3, unpack, 0)

    for t in range(2):
        each(NP, lambda d: leg1(t)(d).wait_send())
        each(NY, lambda d: leg2(t)(d).wait_send())
        each(NP, lambda d: leg3(t)(d).wait_send())
        each(NX, lambda d: cross(t)(d).wait_send())
    for copy in swap:
        copy.wait_send()
    each(NZ, lambda d: tok_a1(d).wait_send())
    each(NY, lambda d: tok_b1(d).wait_send())
    each(NY, lambda d: tok_a2(d).wait_send())
    each(NZ, lambda d: tok_b2(d).wait_send())
    each(NX, lambda d: gates_out(d).wait_send())
    each(NX, lambda d: gates_back(d).wait_send())
    each(NP, lambda d: len1(d).wait_send())
    each(NY, lambda d: len2(d).wait_send())

    each(NY, lambda d: sum_a1(d).wait_recv())
    total = adst[0].astype(F32)
    for p in range(1, NY):
        total = total + adst[p].astype(F32)
    acc[...] = total
    for p in range(NZ):
        aq[p] = acc[T * p : T * p + T, :].astype(BF16)
    each(NZ, lambda d: sum_a2(d).start())
    ar[z] = aq[z]
    each(NZ, lambda d: sum_b1(d).wait_recv())
    total = bdst[0].astype(F32)
    for p in range(1, NZ):
        total = total + bdst[p].astype(F32)
    acc[...] = total
    for p in range(NY):
        bq[p] = acc[T * p : T * p + T, :].astype(BF16)
    each(NY, lambda d: sum_b2(d).start())
    br[y] = bq[y]
    each(NY, lambda d: sum_a1(d).wait_send())
    each(NZ, lambda d: sum_b1(d).wait_send())
    each(NZ, lambda d: sum_a2(d).wait_recv())
    total = ar[0].astype(F32)
    for p in range(1, NZ):
        total = total + ar[p].astype(F32)
    mixed[:, 0:W] = (total * scales[2]).astype(BF16)
    each(NY, lambda d: sum_b2(d).wait_recv())
    total = br[0].astype(F32)
    for p in range(1, NY):
        total = total + br[p].astype(F32)
    mixed[:, W:D] = (total * scales[2]).astype(BF16)
    each(NZ, lambda d: sum_a2(d).wait_send())
    each(NY, lambda d: sum_b2(d).wait_send())


def solution(mesh):
    rows, NX = mesh.shape["row"], mesh.shape["col"]
    NZ = math.isqrt(rows // 2)
    NY = rows // 2 // NZ
    NP = 2 * NZ

    def per_device(tokens, gate_weight, up_weight, down_weight, u_init, gammas):
        T, D = tokens.shape
        H = gate_weight.shape[0]
        ZT = NZ * T
        NT = NY * ZT
        XT = NT // NX
        W = D // 2
        YT = NY * T
        dims = (NX, NY, NZ, H, D, T, D * NX, H * rows)
        V = pltpu.VMEM
        dma = pltpu.SemaphoreType.DMA
        anywhere = pl.BlockSpec(memory_space=pl.ANY)
        vmem = pl.BlockSpec(memory_space=pltpu.VMEM)
        return pl.pallas_call(
            functools.partial(kernel, dims),
            out_shape=(
                V((T, D), BF16),
                V((3, H), F32),
                V((3, D), F32),
            ),
            in_specs=[anywhere] * 6,
            out_specs=(vmem, vmem, vmem),
            scratch_shapes=[
                pltpu.SMEM((3,), F32),
                V((3, H, D), F32), V((4 * H, D), BF16), V((2 * H, D), BF16), V((3, H), F32),
                V((NZ, T, W), BF16), V((NY, T, W), BF16), V((ZT, W), F32),
                V((NY, ZT, W), BF16), V((NZ, YT, W), BF16), V((NT, W), F32), V((NT, D), BF16), V((NT, NT), BF16),
                V((2, 4, D), F32), V((2, NP, 4, 128), F32), V((2, 4, 128), F32),
                V((2, NY, 4, 128), F32), V((2, 4, 128), F32), V((2, 4, D), F32), V((3, D), F32),
                V((2, 8, 128), F32), V((2, NX, 8, 128), F32),
                V((1, 128), F32), V((NP, 1, 128), F32), V((1, 128), F32), V((NY, 1, 128), F32),
                V((NT, 4 * H), F32), V((NX, XT, 4 * H), F32), V((NT, 4 * H), F32), V((NT, 2 * H), BF16),
                V((NY, ZT, W), BF16), V((NY, ZT, W), BF16), V((NZ, YT, W), BF16), V((NZ, YT, W), BF16), V((ZT, W), F32),
                V((NZ, T, W), BF16), V((NZ, T, W), BF16), V((NY, T, W), BF16), V((NY, T, W), BF16),
                dma((3,)), dma((4,)),
                dma((2, NP)), dma((2, NP)), dma((2, NY)), dma((2, NY)), dma((2, NP)), dma((2, NP)),
                dma((2, NX)), dma((2, NX)),
                dma((NP,)), dma((NP,)), dma((NY,)), dma((NY,)), dma((3,)), dma((3,)),
                dma((NZ,)), dma((NZ,)), dma((NY,)), dma((NY,)), dma((NY,)), dma((NY,)), dma((NZ,)), dma((NZ,)),
                dma((NX,)), dma((NX,)), dma((NX,)), dma((NX,)),
                dma((NY,)), dma((NY,)), dma((NZ,)), dma((NZ,)), dma((NZ,)), dma((NZ,)), dma((NY,)), dma((NY,)),
            ],
            compiler_params=pltpu.CompilerParams(
                collective_id=0, has_side_effects=True, vmem_limit_bytes=60 * 1024 * 1024
            ),
        )(tokens, gate_weight, up_weight, down_weight, u_init, gammas)

    return jax.shard_map(
        per_device,
        mesh=mesh,
        in_specs=(
            P("row", "col"),
            P("row", "col"),
            P("row", "col"),
            P("row", "col"),
            P(None, "row"),
            P(),
        ),
        out_specs=(P("row", "col"), P(None, "row"), P(None, "col")),
        check_vma=False,
    )
```

```python
import functools
import math

import jax
import jax.numpy as jnp
from jax import lax
from jax.experimental import pallas as pl
from jax.experimental.pallas import tpu as pltpu
from jax.sharding import PartitionSpec as P

MESH = pl.DeviceIdType.MESH
EPS = 1e-06
F32 = jnp.float32
BF16 = jnp.bfloat16


def kernel(
    dims,
    tok_h, wg_h, wu_h, wd_h, ui_h, gam_h,
    mixed, uout, vout,
    gam, w, w16, d16, ui, ta, tb, tzf, xa, xb, xf, x16, perm,
    part_0, r1b_0, r1s_0, r2b_0, r2s_0, bv_0, bn_0, pk_0, cb_0, s3_0, r3b_0, s4_0, r4b_0,
    part_1, r1b_1, r1s_1, r2b_1, r2s_1, bv_1, bn_1, pk_1, cb_1, s3_1, r3b_1, s4_1, r4b_1,
    gp, xr, ga, hid, asrc, adst, bsrc, bdst, acc, aq, ar, bq, br,
    wsem, lsem, p1s, p1r, p2s, p2r, p3s, p3r, cs, cr,
    e1s, e1r, e2s, e2r, ks, kr, ta1s, ta1r, tb1s, tb1r, ta2s, ta2r, tb2s, tb2r,
    gs, gr, hs, hr, as1, ar1, bs1, br1, as2, ar2, bs2, br2,
):
    NX, NY, NZ, H, D, T, DT, FT = dims
    FIRST, N, ROWS = (0, 1), (1, 2), (2, 4)
    part, r1b, r1s, r2b, r2s = (part_0, part_1), (r1b_0, r1b_1), (r1s_0, r1s_1), (r2b_0, r2b_1), (r2s_0, r2s_1)
    bv, bn, pk, cb = (bv_0, bv_1), (bn_0, bn_1), (pk_0, pk_1), (cb_0, cb_1)
    s3, r3b, s4, r4b = (s3_0, s3_1), (r3b_0, r3b_1), (s4_0, s4_1), (r4b_0, r4b_1)
    NP = 2 * NZ
    HB = H // 8
    ZT = NZ * T
    YT = NY * T
    XT = NY * ZT // NX
    W = D // 2
    row = lax.axis_index("row")
    x = lax.axis_index("col")
    y = row // NP
    q = lax.rem(row, NP)
    z = q // 2
    c = lax.rem(q, 2)

    def remote(src, dst, ssem, rsem, r, cc):
        return pltpu.make_async_remote_copy(
            src_ref=src, dst_ref=dst, send_sem=ssem, recv_sem=rsem,
            device_id={"row": r, "col": cc}, device_id_type=MESH,
        )

    def each(n, fn):
        def body(d, carry):
            fn(d)
            return carry
        lax.fori_loop(1, n, body, 0)

    def plane(d):
        p = lax.rem(q + d, NP)
        return p, y * NP + p

    def along_y(d):
        p = lax.rem(y + d, NY)
        return p, p * NP + q

    def along_z(d):
        p = lax.rem(z + d, NZ)
        return p, y * NP + p * 2 + c

    def along_x(d):
        return lax.rem(x + d, NX)

    def lanes(p, n=128):
        return pl.ds(pl.multiple_of(p * n, n), n)

    barrier = pltpu.get_barrier_semaphore()

    def greet(r, cc):
        pl.semaphore_signal(
            barrier, inc=1, device_id={"row": r, "col": cc}, device_id_type=MESH
        )

    each(NP, lambda d: greet(plane(d)[1], x))
    each(NY, lambda d: greet(along_y(d)[1], x))
    each(NX, lambda d: greet(row, along_x(d)))

    loads = [
        pltpu.make_async_copy(ui_h, ui, lsem.at[0]),
        pltpu.make_async_copy(wg_h, w.at[0], wsem.at[0]),
        pltpu.make_async_copy(wu_h, w.at[1], wsem.at[1]),
        pltpu.make_async_copy(wd_h, w.at[2], wsem.at[2]),
        pltpu.make_async_copy(tok_h.at[:, 0:W], ta.at[z], lsem.at[1]),
        pltpu.make_async_copy(tok_h.at[:, W:D], tb.at[y], lsem.at[2]),
        pltpu.make_async_copy(gam_h, gam, lsem.at[3]),
    ]
    for load in loads:
        load.start()

    lane = lax.broadcasted_iota(jnp.int32, (8, 128), 1)
    lane1 = lax.broadcasted_iota(jnp.int32, (1, 128), 1)
    hl = lax.broadcasted_iota(jnp.int32, (8, H), 1)
    hs_ = lax.broadcasted_iota(jnp.int32, (8, H), 0)
    diag = hl - hs_

    def spread(values):
        out = jnp.zeros((1, 128), F32)
        for k, value in enumerate(values):
            out = jnp.where(lane1 == k, value, out)
        return out

    def per_block(values):
        out = values[-1]
        for k in reversed(range(len(values) - 1)):
            out = jnp.where(lane1 < (k + 1) * HB, values[k], out)
        return out

    def pick(vector, k):
        return vector[:, k : k + 1]

    def back_first(g):
        def body(j, carry):
            k = FIRST[g] + j
            pltpu.make_async_copy(w.at[k], w.at[k], wsem.at[k]).wait()
            left = jnp.broadcast_to(ui[pl.ds(k, 1), :], (8, H))
            total = jnp.zeros((8, D), F32)
            for rb in range(HB):
                col = jnp.sum(jnp.where(diag == 8 * rb, left, 0.0), axis=1, keepdims=True)
                total = total + w[k, 8 * rb : 8 * rb + 8, :] * col
            part[g][0, pl.ds(j, 1), :] = jnp.sum(total, axis=0, keepdims=True)
            return carry
        lax.fori_loop(0, N[g], body, 0)
        part[g][0, N[g] : ROWS[g], :] = jnp.zeros((ROWS[g] - N[g], D), F32)

    def back_second(g, fore, squares):
        def body(j, carry):
            left = pltpu.roll(fore, lax.rem(128 - j * HB, 128), 1)
            total = jnp.zeros((8, D), F32)
            for rb in range(HB):
                total = total + w[FIRST[g] + j, 8 * rb : 8 * rb + 8, :] * left[:, rb : rb + 1]
            part[g][1, pl.ds(j, 1), :] = jnp.sum(total, axis=0, keepdims=True)
            return carry
        lax.fori_loop(0, N[g], body, 0)
        line = jnp.broadcast_to(spread(squares), (ROWS[g] - N[g], 128))
        for p in range(NP):
            part[g][1, N[g] : ROWS[g], 128 * p : 128 * p + 128] = line

    def fore_packed(g, source):
        def body(j, packed):
            b = source[pl.ds(j, 1), :]
            b8 = jnp.broadcast_to(b, (8, D))
            mine = jnp.zeros((8, 128), F32)
            for rb in range(HB):
                got = jnp.sum(w[FIRST[g] + j, 8 * rb : 8 * rb + 8, :] * b8, axis=1, keepdims=True)
                mine = jnp.where(lane == rb, got, mine)
            packed = packed + pltpu.roll(mine, j * HB, 1)
            square = jnp.sum(b * b, axis=1, keepdims=True)
            return jnp.where(lane == N[g] * HB + j, square, packed)
        return lax.fori_loop(0, N[g], body, jnp.zeros((8, 128), F32))

    def leg1(g, t):
        return lambda d: remote(
            part[g].at[t, :, lanes(plane(d)[0])], r1b[g].at[t, q],
            p1s.at[g, t, d], p1r.at[g, t, d], plane(d)[1], x,
        )

    def leg2(g, t):
        return lambda d: remote(
            r1s[g].at[t], r2b[g].at[t, y], p2s.at[g, t, d], p2r.at[g, t, d], along_y(d)[1], x
        )

    def leg3(g, t):
        return lambda d: remote(
            r2s[g].at[t], bv[g].at[t, :, lanes(q)], p3s.at[g, t, d], p3r.at[g, t, d], plane(d)[1], x
        )

    def start1(g, t):
        each(NP, lambda d: leg1(g, t)(d).start())
        r1b[g][t, q] = part[g][t, :, lanes(q)]

    def start2(g, t):
        each(NP, lambda d: leg1(g, t)(d).wait_recv())
        total = r1b[g][t, 0]
        for p in range(1, NP):
            total = total + r1b[g][t, p]
        r1s[g][t] = total
        each(NY, lambda d: leg2(g, t)(d).start())
        r2b[g][t, y] = total

    def start3(g, t):
        each(NY, lambda d: leg2(g, t)(d).wait_recv())
        total = r2b[g][t, 0]
        for p in range(1, NY):
            total = total + r2b[g][t, p]
        r2s[g][t] = total
        each(NP, lambda d: leg3(g, t)(d).start())
        bv[g][t, :, lanes(q)] = total

    def finish3(g, t):
        each(NP, lambda d: leg3(g, t)(d).wait_recv())

    def normalise(g):
        line = bv[g][1, N[g] : N[g] + 1, 0:128]
        for j in range(N[g]):
            bn[g][j : j + 1, :] = bv[g][1, j : j + 1, :] / jnp.sqrt(pick(line, j) / FT + EPS)

    def cross(g, t):
        return lambda d: remote(
            pk[g].at[t], cb[g].at[t, x], cs.at[g, t, d], cr.at[g, t, d], row, along_x(d)
        )

    def col_start(g, t, packed):
        pk[g][t] = packed
        each(NX, lambda d: cross(g, t)(d).start())
        cb[g][t, x] = packed

    def col_finish(g, t):
        each(NX, lambda d: cross(g, t)(d).wait_recv())
        total = cb[g][t, 0]
        for p in range(1, NX):
            total = total + cb[g][t, p]
        base = N[g] * HB
        roots = [
            jnp.sqrt(total[0:1, base + j : base + j + 1] / DT + EPS) for j in range(N[g])
        ]
        fore = jnp.where(lane < base, total / per_block(roots), 0.0)
        squares = []
        for j in range(N[g]):
            own = jnp.where((lane >= j * HB) & (lane < (j + 1) * HB), fore * fore, 0.0)
            own = jnp.sum(own, axis=1, keepdims=True)
            squares.append(jnp.sum(own, axis=0, keepdims=True))
        return fore, squares, roots

    def len1(g):
        return lambda d: remote(
            s3[g], r3b[g].at[q], e1s.at[g, d], e1r.at[g, d], plane(d)[1], x
        )

    def len2(g):
        return lambda d: remote(
            s4[g], r4b[g].at[y], e2s.at[g, d], e2r.at[g, d], along_y(d)[1], x
        )

    def lengths_start(g, squares):
        line = spread(squares)
        s3[g][...] = line
        each(NP, lambda d: len1(g)(d).start())
        r3b[g][q] = line

    def lengths_turn(g):
        each(NP, lambda d: len1(g)(d).wait_recv())
        line = r3b[g][0]
        for p in range(1, NP):
            line = line + r3b[g][p]
        s4[g][...] = line
        each(NY, lambda d: len2(g)(d).start())
        r4b[g][y] = line

    def lengths_finish(g):
        each(NY, lambda d: len2(g)(d).wait_recv())
        line = r4b[g][0]
        for p in range(1, NY):
            line = line + r4b[g][p]
        lengths = [jnp.sqrt(pick(line, j) / FT + EPS) for j in range(N[g])]
        sigmas = [pick(line, j) / lengths[j] / math.sqrt(FT * DT) for j in range(N[g])]
        return lengths, [gam[FIRST[g] + j] / sigmas[j] for j in range(N[g])]

    def left_out(g, fore, lengths):
        left = fore / per_block(lengths)
        keep = (diag >= 0) & (lax.rem(diag, 8) == 0)

        def unpack(j, carry):
            own = pltpu.roll(left, lax.rem(128 - j * HB, 128), 1)
            rows = jnp.zeros((8, H), F32)
            for rb in range(HB):
                rows = jnp.where(diag == 8 * rb, own[:, rb : rb + 1], rows)
            rows = jnp.where(keep, rows, 0.0)
            uout[pl.ds(FIRST[g] + j, 1), :] = jnp.sum(rows, axis=0, keepdims=True)
            return carry

        lax.fori_loop(0, N[g], unpack, 0)

    def right_out(g, roots):
        for j in range(N[g]):
            vout[FIRST[g] + j : FIRST[g] + j + 1, :] = bn[g][j : j + 1, :] / roots[j]

    swap = [
        remote(w16.at[pl.ds(pl.multiple_of(c * H, H), H)], w16.at[pl.ds(pl.multiple_of(c * H, H), H)],
               ks.at[0], kr.at[0], row + 1 - 2 * c, x),
        remote(w16.at[pl.ds(pl.multiple_of((2 + c) * H, H), H)], w16.at[pl.ds(pl.multiple_of((2 + c) * H, H), H)],
               ks.at[1], kr.at[1], row + 1 - 2 * c, x),
        remote(d16.at[pl.ds(pl.multiple_of(c * H, H), H)], d16.at[pl.ds(pl.multiple_of(c * H, H), H)],
               ks.at[2], kr.at[2], row + 1 - 2 * c, x),
    ]

    def tok_a1(d):
        return remote(tok_h.at[:, 0:W], ta.at[z], ta1s.at[d], ta1r.at[d], along_z(d)[1], x)

    def tok_b1(d):
        return remote(tok_h.at[:, W:D], tb.at[y], tb1s.at[d], tb1r.at[d], along_y(d)[1], x)

    def tok_a2(d):
        return remote(xa.at[y], xa.at[y], ta2s.at[d], ta2r.at[d], along_y(d)[1], x)

    def tok_b2(d):
        return remote(xb.at[z], xb.at[z], tb2s.at[d], tb2r.at[d], along_z(d)[1], x)

    def gates_out(d):
        return remote(
            gp.at[pl.ds(pl.multiple_of(along_x(d) * XT, XT), XT)], xr.at[x],
            gs.at[d], gr.at[d], row, along_x(d),
        )

    def gates_back(d):
        mine = ga.at[pl.ds(pl.multiple_of(x * XT, XT), XT)]
        return remote(mine, mine, hs.at[d], hr.at[d], row, along_x(d))

    def sum_a1(d):
        return remote(asrc.at[along_y(d)[0]], adst.at[y], as1.at[d], ar1.at[d], along_y(d)[1], x)

    def sum_b1(d):
        return remote(bsrc.at[along_z(d)[0]], bdst.at[z], bs1.at[d], br1.at[d], along_z(d)[1], x)

    def sum_a2(d):
        return remote(aq.at[along_z(d)[0]], ar.at[z], as2.at[d], ar2.at[d], along_z(d)[1], x)

    def sum_b2(d):
        return remote(bq.at[along_y(d)[0]], br.at[y], bs2.at[d], br2.at[d], along_y(d)[1], x)

    loads[0].wait()
    back_first(0)
    back_first(1)
    pl.semaphore_wait(barrier, (NP - 1) + (NY - 1) + (NX - 1))
    start1(0, 0)
    start1(1, 0)
    each(NZ, lambda d: tok_a1(d).start())
    each(NY, lambda d: tok_b1(d).start())
    w16[pl.ds(pl.multiple_of(c * H, H), H), :] = w[0].astype(BF16)
    w16[pl.ds(pl.multiple_of((2 + c) * H, H), H), :] = w[1].astype(BF16)
    d16[pl.ds(pl.multiple_of(c * H, H), H), :] = w[2].astype(BF16)
    start2(0, 0)
    start2(1, 0)

    loads[4].wait()
    each(NZ, lambda d: tok_a1(d).wait_recv())
    for p in range(NZ):
        tzf[T * p : T * p + T, :] = ta[p].astype(F32)
    xa[y] = tzf[...].astype(BF16)
    each(NY, lambda d: tok_a2(d).start())
    loads[5].wait()
    each(NY, lambda d: tok_b1(d).wait_recv())
    for p in range(NY):
        tzf[T * p : T * p + T, :] = tb[p].astype(F32)
    xb[z] = tzf[...].astype(BF16)
    lo = lax.broadcasted_iota(jnp.int32, (NY * ZT, NY * ZT), 0)
    hi = lax.broadcasted_iota(jnp.int32, (NY * ZT, NY * ZT), 1)
    major = jnp.zeros_like(lo)
    for p in range(1, NY):
        major = major + (lo >= p * ZT).astype(jnp.int32)
    minor = jnp.zeros_like(lo)
    for p in range(1, NZ):
        minor = minor + (lo - major * ZT >= p * T).astype(jnp.int32)
    wanted = minor * YT + major * T + (lo - major * ZT - minor * T)
    perm[...] = jnp.where(hi == wanted, 1.0, 0.0).astype(BF16)
    start3(0, 0)
    start3(1, 0)
    each(NZ, lambda d: tok_b2(d).start())
    finish3(0, 0)
    col_start(0, 0, fore_packed(0, bv[0].at[0]))
    finish3(1, 0)
    col_start(1, 0, fore_packed(1, bv[1].at[0]))
    for copy in swap:
        copy.start()
    fore, squares, _ = col_finish(0, 0)
    back_second(0, fore, squares)
    start1(0, 1)
    fore, squares, _ = col_finish(1, 0)
    back_second(1, fore, squares)
    start1(1, 1)

    each(NY, lambda d: tok_a2(d).wait_recv())
    for p in range(NY):
        xf[ZT * p : ZT * p + ZT, :] = xa[p].astype(F32)
    x16[:, 0:W] = xf[...].astype(BF16)
    each(NZ, lambda d: tok_b2(d).wait_recv())
    for p in range(NZ):
        xf[YT * p : YT * p + YT, :] = xb[p].astype(F32)
    x16[:, W:D] = jnp.dot(
        perm[...], xf[...].astype(BF16), preferred_element_type=F32
    ).astype(BF16)
    swap[0].wait_recv()
    swap[1].wait_recv()
    gp[...] = lax.dot_general(
        x16[...], w16[...], (((1,), (1,)), ((), ())), preferred_element_type=F32
    )
    each(NX, lambda d: gates_out(d).start())
    xr[x] = gp[pl.ds(pl.multiple_of(x * XT, XT), XT), :]

    start2(0, 1)
    start2(1, 1)
    start3(0, 1)
    start3(1, 1)
    each(NX, lambda d: gates_out(d).wait_recv())
    total = xr[0]
    for p in range(1, NX):
        total = total + xr[p]
    ga[pl.ds(pl.multiple_of(x * XT, XT), XT), :] = total
    finish3(0, 1)
    normalise(0)
    col_start(0, 1, fore_packed(0, bn[0]))
    finish3(1, 1)
    normalise(1)
    col_start(1, 1, fore_packed(1, bn[1]))
    each(NX, lambda d: gates_back(d).start())
    fore_0, squares, roots_0 = col_finish(0, 1)
    lengths_start(0, squares)
    fore_1, squares, roots_1 = col_finish(1, 1)
    lengths_start(1, squares)
    right_out(0, roots_0)
    right_out(1, roots_1)
    lengths_turn(0)
    lengths_turn(1)
    swap[2].wait_recv()
    each(NX, lambda d: gates_back(d).wait_recv())
    loads[6].wait()
    lengths_0, scales_0 = lengths_finish(0)
    gate = ga[:, 0 : 2 * H] * scales_0[0]
    upper = ga[:, 2 * H : 4 * H]
    hid[...] = (gate * jax.nn.sigmoid(gate) * upper).astype(BF16)

    out = jnp.dot(hid[...], d16[:, 0:W], preferred_element_type=F32)
    for p in range(NY):
        asrc[p] = out[ZT * p : ZT * p + ZT].astype(BF16)
    each(NY, lambda d: sum_a1(d).start())
    turned = jnp.dot(perm[...], hid[...], preferred_element_type=F32).astype(BF16)
    out = jnp.dot(turned, d16[:, W:D], preferred_element_type=F32)
    for p in range(NZ):
        bsrc[p] = out[YT * p : YT * p + YT].astype(BF16)
    each(NZ, lambda d: sum_b1(d).start())
    adst[y] = asrc[y]
    bdst[z] = bsrc[z]

    lengths_1, scales_1 = lengths_finish(1)
    left_out(0, fore_0, lengths_0)
    left_out(1, fore_1, lengths_1)

    for g in range(2):
        for t in range(2):
            each(NP, lambda d: leg1(g, t)(d).wait_send())
            each(NY, lambda d: leg2(g, t)(d).wait_send())
            each(NP, lambda d: leg3(g, t)(d).wait_send())
            each(NX, lambda d: cross(g, t)(d).wait_send())
        each(NP, lambda d: len1(g)(d).wait_send())
        each(NY, lambda d: len2(g)(d).wait_send())
    for copy in swap:
        copy.wait_send()
    each(NZ, lambda d: tok_a1(d).wait_send())
    each(NY, lambda d: tok_b1(d).wait_send())
    each(NY, lambda d: tok_a2(d).wait_send())
    each(NZ, lambda d: tok_b2(d).wait_send())
    each(NX, lambda d: gates_out(d).wait_send())
    each(NX, lambda d: gates_back(d).wait_send())

    each(NY, lambda d: sum_a1(d).wait_recv())
    total = adst[0].astype(F32)
    for p in range(1, NY):
        total = total + adst[p].astype(F32)
    acc[...] = total
    for p in range(NZ):
        aq[p] = acc[T * p : T * p + T, :].astype(BF16)
    each(NZ, lambda d: sum_a2(d).start())
    ar[z] = aq[z]
    each(NZ, lambda d: sum_b1(d).wait_recv())
    total = bdst[0].astype(F32)
    for p in range(1, NZ):
        total = total + bdst[p].astype(F32)
    acc[...] = total
    for p in range(NY):
        bq[p] = acc[T * p : T * p + T, :].astype(BF16)
    each(NY, lambda d: sum_b2(d).start())
    br[y] = bq[y]
    each(NY, lambda d: sum_a1(d).wait_send())
    each(NZ, lambda d: sum_b1(d).wait_send())
    each(NZ, lambda d: sum_a2(d).wait_recv())
    total = ar[0].astype(F32)
    for p in range(1, NZ):
        total = total + ar[p].astype(F32)
    mixed[:, 0:W] = (total * scales_1[0] * scales_1[1]).astype(BF16)
    each(NY, lambda d: sum_b2(d).wait_recv())
    total = br[0].astype(F32)
    for p in range(1, NY):
        total = total + br[p].astype(F32)
    mixed[:, W:D] = (total * scales_1[0] * scales_1[1]).astype(BF16)
    each(NZ, lambda d: sum_a2(d).wait_send())
    each(NY, lambda d: sum_b2(d).wait_send())


def hand_over(a, b, c, d, e, f, sems):
    copies = [
        pltpu.make_async_copy(source, target, sems.at[i])
        for i, (source, target) in enumerate(((a, d), (b, e), (c, f)))
    ]
    for copy in copies:
        copy.start()
    for copy in copies:
        copy.wait()


def solution(mesh):
    rows, NX = mesh.shape["row"], mesh.shape["col"]
    NZ = math.isqrt(rows // 2)
    NY = rows // 2 // NZ
    NP = 2 * NZ

    def per_device(tokens, gate_weight, up_weight, down_weight, u_init, gammas):
        T, D = tokens.shape
        H = gate_weight.shape[0]
        ZT = NZ * T
        NT = NY * ZT
        XT = NT // NX
        W = D // 2
        YT = NY * T
        dims = (NX, NY, NZ, H, D, T, D * NX, H * rows)
        V = pltpu.VMEM
        dma = pltpu.SemaphoreType.DMA

        def group(rows, n):
            return [
                V((2, rows, D), F32), V((2, NP, rows, 128), F32), V((2, rows, 128), F32),
                V((2, NY, rows, 128), F32), V((2, rows, 128), F32), V((2, rows, D), F32), V((n, D), F32),
                V((2, 8, 128), F32), V((2, NX, 8, 128), F32),
                V((1, 128), F32), V((NP, 1, 128), F32), V((1, 128), F32), V((NY, 1, 128), F32),
            ]

        anywhere = pl.BlockSpec(memory_space=pl.ANY)
        vmem = pl.BlockSpec(memory_space=pltpu.VMEM)
        held = pl.pallas_call(
            functools.partial(kernel, dims),
            out_shape=(
                V((T, D), BF16),
                V((3, H), F32),
                V((3, D), F32),
            ),
            in_specs=[anywhere] * 6,
            out_specs=(vmem, vmem, vmem),
            scratch_shapes=[
                pltpu.SMEM((3,), F32),
                V((3, H, D), F32), V((4 * H, D), BF16), V((2 * H, D), BF16), V((3, H), F32),
                V((NZ, T, W), BF16), V((NY, T, W), BF16), V((ZT, W), F32),
                V((NY, ZT, W), BF16), V((NZ, YT, W), BF16), V((NT, W), F32), V((NT, D), BF16), V((NT, NT), BF16),
                *(ref for g in range(2) for ref in group((2, 4)[g], (1, 2)[g])),
                V((NT, 4 * H), F32), V((NX, XT, 4 * H), F32), V((NT, 4 * H), F32), V((NT, 2 * H), BF16),
                V((NY, ZT, W), BF16), V((NY, ZT, W), BF16), V((NZ, YT, W), BF16), V((NZ, YT, W), BF16), V((ZT, W), F32),
                V((NZ, T, W), BF16), V((NZ, T, W), BF16), V((NY, T, W), BF16), V((NY, T, W), BF16),
                dma((3,)), dma((4,)),
                dma((2, 2, NP)), dma((2, 2, NP)), dma((2, 2, NY)), dma((2, 2, NY)), dma((2, 2, NP)), dma((2, 2, NP)),
                dma((2, 2, NX)), dma((2, 2, NX)),
                dma((2, NP)), dma((2, NP)), dma((2, NY)), dma((2, NY)), dma((3,)), dma((3,)),
                dma((NZ,)), dma((NZ,)), dma((NY,)), dma((NY,)), dma((NY,)), dma((NY,)), dma((NZ,)), dma((NZ,)),
                dma((NX,)), dma((NX,)), dma((NX,)), dma((NX,)),
                dma((NY,)), dma((NY,)), dma((NZ,)), dma((NZ,)), dma((NZ,)), dma((NZ,)), dma((NY,)), dma((NY,)),
            ],
            compiler_params=pltpu.CompilerParams(
                collective_id=0, has_side_effects=True, vmem_limit_bytes=60 * 1024 * 1024
            ),
        )(tokens, gate_weight, up_weight, down_weight, u_init, gammas)
        return pl.pallas_call(
            hand_over,
            out_shape=tuple(jax.ShapeDtypeStruct(v.shape, v.dtype) for v in held),
            in_specs=[vmem] * 3,
            out_specs=(anywhere,) * 3,
            scratch_shapes=[dma((3,))],
            compiler_params=pltpu.CompilerParams(vmem_limit_bytes=1024 * 1024),
        )(*held)

    return jax.shard_map(
        per_device,
        mesh=mesh,
        in_specs=(
            P("row", "col"),
            P("row", "col"),
            P("row", "col"),
            P("row", "col"),
            P(None, "row"),
            P(),
        ),
        out_specs=(P("row", "col"), P(None, "row"), P(None, "col")),
        check_vma=False,
    )
```

```python
import functools
import math

import jax
import jax.numpy as jnp
from jax import lax
from jax.experimental import pallas as pl
from jax.experimental.pallas import tpu as pltpu
from jax.sharding import PartitionSpec as P

MESH = pl.DeviceIdType.MESH
EPS = 1e-06
F32 = jnp.float32
BF16 = jnp.bfloat16


def kernel(
    dims,
    tok_h, wg_h, wu_h, wd_h, ui_h, gam_h,
    mixed, uout, vout,
    gam, w, w16, d16, ui, ta, tb, tzf, xa, xb, xf, x16, perm,
    part_0, r1b_0, r1s_0, r2b_0, r2s_0, bv_0, bn_0, pk_0, cb_0, s3_0, r3b_0, s4_0, r4b_0,
    part_1, r1b_1, r1s_1, r2b_1, r2s_1, bv_1, bn_1, pk_1, cb_1, s3_1, r3b_1, s4_1, r4b_1,
    gp, xr, ga, hid, asrc, adst, bsrc, bdst, acc, acb, aq, ar, bq, br,
    wsem, lsem, p1s, p1r, p2s, p2r, p3s, p3r, cs, cr,
    e1s, e1r, e2s, e2r, ks, kr, ta1s, ta1r, tb1s, tb1r, ta2s, ta2r, tb2s, tb2r,
    gs, gr, hs, hr, as1, ar1, bs1, br1, as2, ar2, bs2, br2,
):
    NX, NY, NZ, H, D, T, DT, FT = dims
    FIRST, N, ROWS = (0, 1), (1, 2), (2, 4)
    part, r1b, r1s, r2b, r2s = (part_0, part_1), (r1b_0, r1b_1), (r1s_0, r1s_1), (r2b_0, r2b_1), (r2s_0, r2s_1)
    bv, bn, pk, cb = (bv_0, bv_1), (bn_0, bn_1), (pk_0, pk_1), (cb_0, cb_1)
    s3, r3b, s4, r4b = (s3_0, s3_1), (r3b_0, r3b_1), (s4_0, s4_1), (r4b_0, r4b_1)
    NP = 2 * NZ
    HB = H // 8
    ZT = NZ * T
    YT = NY * T
    XT = NY * ZT // NX
    W = D // 2
    Q = W // 2
    row = lax.axis_index("row")
    x = lax.axis_index("col")
    y = row // NP
    q = row & (NP - 1)
    z = q // 2
    c = q & 1

    def remote(src, dst, ssem, rsem, r, cc):
        return pltpu.make_async_remote_copy(
            src_ref=src, dst_ref=dst, send_sem=ssem, recv_sem=rsem,
            device_id={"row": r, "col": cc}, device_id_type=MESH,
        )

    def each(n, fn):
        for d in sorted(range(1, n), key=lambda d: -min(d, n - d)):
            fn(d)

    def turn(at, d, n):
        return (at + d) & (n - 1)

    def plane(d):
        p = turn(q, d, NP)
        return p, y * NP + p

    def along_y(d):
        p = turn(y, d, NY)
        return p, p * NP + q

    def along_z(d):
        p = turn(z, d, NZ)
        return p, y * NP + p * 2 + c

    def along_x(d):
        return turn(x, d, NX)

    def lanes(p, n=128):
        return pl.ds(pl.multiple_of(p * n, n), n)

    barrier = pltpu.get_barrier_semaphore()

    def greet(r, cc):
        pl.semaphore_signal(
            barrier, inc=1, device_id={"row": r, "col": cc}, device_id_type=MESH
        )

    each(NY, lambda d: greet(along_y(d)[1], x))
    each(NP, lambda d: greet(plane(d)[1], x))
    each(NX, lambda d: greet(row, along_x(d)))

    loads = [
        pltpu.make_async_copy(ui_h, ui, lsem.at[0]),
        pltpu.make_async_copy(wg_h, w.at[0], wsem.at[0]),
        pltpu.make_async_copy(wu_h, w.at[1], wsem.at[1]),
        pltpu.make_async_copy(wd_h, w.at[2], wsem.at[2]),
        pltpu.make_async_copy(tok_h.at[:, 0:W], ta.at[z], lsem.at[1]),
        pltpu.make_async_copy(tok_h.at[:, W:D], tb.at[y], lsem.at[2]),
        pltpu.make_async_copy(gam_h, gam, lsem.at[3]),
    ]
    for load in loads:
        load.start()

    lane = lax.broadcasted_iota(jnp.int32, (8, 128), 1)
    lane1 = lax.broadcasted_iota(jnp.int32, (1, 128), 1)
    hl = lax.broadcasted_iota(jnp.int32, (8, H), 1)
    hs_ = lax.broadcasted_iota(jnp.int32, (8, H), 0)
    diag = hl - hs_

    def spread(values):
        out = jnp.zeros((1, 128), F32)
        for k, value in enumerate(values):
            out = jnp.where(lane1 == k, value, out)
        return out

    def per_block(values):
        out = values[-1]
        for k in reversed(range(len(values) - 1)):
            out = jnp.where(lane1 < (k + 1) * HB, values[k], out)
        return out

    def pick(vector, k):
        return vector[:, k : k + 1]

    def back_first(g):
        def body(j, carry):
            k = FIRST[g] + j
            pltpu.make_async_copy(w.at[k], w.at[k], wsem.at[k]).wait()
            left = jnp.broadcast_to(ui[pl.ds(k, 1), :], (8, H))
            total = jnp.zeros((8, D), F32)
            for rb in range(HB):
                col = jnp.sum(jnp.where(diag == 8 * rb, left, 0.0), axis=1, keepdims=True)
                total = total + w[k, 8 * rb : 8 * rb + 8, :] * col
            part[g][0, pl.ds(j, 1), :] = jnp.sum(total, axis=0, keepdims=True)
            return carry
        lax.fori_loop(0, N[g], body, 0)
        part[g][0, N[g] : ROWS[g], :] = jnp.zeros((ROWS[g] - N[g], D), F32)

    def back_second(g, fore, squares):
        def body(j, carry):
            left = pltpu.roll(fore, lax.rem(128 - j * HB, 128), 1)
            total = jnp.zeros((8, D), F32)
            for rb in range(HB):
                total = total + w[FIRST[g] + j, 8 * rb : 8 * rb + 8, :] * left[:, rb : rb + 1]
            part[g][1, pl.ds(j, 1), :] = jnp.sum(total, axis=0, keepdims=True)
            return carry
        lax.fori_loop(0, N[g], body, 0)
        line = jnp.broadcast_to(spread(squares), (ROWS[g] - N[g], 128))
        for p in range(NP):
            part[g][1, N[g] : ROWS[g], 128 * p : 128 * p + 128] = line

    def fore_packed(g, source):
        def body(j, packed):
            b = source[pl.ds(j, 1), :]
            b8 = jnp.broadcast_to(b, (8, D))
            mine = jnp.zeros((8, 128), F32)
            for rb in range(HB):
                got = jnp.sum(w[FIRST[g] + j, 8 * rb : 8 * rb + 8, :] * b8, axis=1, keepdims=True)
                mine = jnp.where(lane == rb, got, mine)
            packed = packed + pltpu.roll(mine, j * HB, 1)
            square = jnp.sum(b * b, axis=1, keepdims=True)
            return jnp.where(lane == N[g] * HB + j, square, packed)
        return lax.fori_loop(0, N[g], body, jnp.zeros((8, 128), F32))

    def leg1(g, t):
        return lambda d: remote(
            part[g].at[t, :, lanes(plane(d)[0])], r1b[g].at[t, q],
            p1s.at[g, t, d], p1r.at[g, t, d], plane(d)[1], x,
        )

    def leg2(g, t):
        return lambda d: remote(
            r1s[g].at[t], r2b[g].at[t, y], p2s.at[g, t, d], p2r.at[g, t, d], along_y(d)[1], x
        )

    def leg3(g, t):
        return lambda d: remote(
            r2s[g].at[t], bv[g].at[t, :, lanes(q)], p3s.at[g, t, d], p3r.at[g, t, d], plane(d)[1], x
        )

    def start1(g, t):
        each(NP, lambda d: leg1(g, t)(d).start())
        r1b[g][t, q] = part[g][t, :, lanes(q)]

    def start2(g, t):
        each(NP, lambda d: leg1(g, t)(d).wait_recv())
        total = r1b[g][t, 0]
        for p in range(1, NP):
            total = total + r1b[g][t, p]
        r1s[g][t] = total
        each(NY, lambda d: leg2(g, t)(d).start())
        r2b[g][t, y] = total

    def start3(g, t):
        each(NY, lambda d: leg2(g, t)(d).wait_recv())
        total = r2b[g][t, 0]
        for p in range(1, NY):
            total = total + r2b[g][t, p]
        r2s[g][t] = total
        each(NP, lambda d: leg3(g, t)(d).start())
        bv[g][t, :, lanes(q)] = total

    def finish3(g, t):
        each(NP, lambda d: leg3(g, t)(d).wait_recv())

    def normalise(g):
        line = bv[g][1, N[g] : N[g] + 1, 0:128]
        for j in range(N[g]):
            bn[g][j : j + 1, :] = bv[g][1, j : j + 1, :] / jnp.sqrt(pick(line, j) / FT + EPS)

    def cross(g, t):
        return lambda d: remote(
            pk[g].at[t], cb[g].at[t, x], cs.at[g, t, d], cr.at[g, t, d], row, along_x(d)
        )

    def col_start(g, t, packed):
        pk[g][t] = packed
        each(NX, lambda d: cross(g, t)(d).start())
        cb[g][t, x] = packed

    def col_finish(g, t):
        each(NX, lambda d: cross(g, t)(d).wait_recv())
        total = cb[g][t, 0]
        for p in range(1, NX):
            total = total + cb[g][t, p]
        base = N[g] * HB
        roots = [
            jnp.sqrt(total[0:1, base + j : base + j + 1] / DT + EPS) for j in range(N[g])
        ]
        fore = jnp.where(lane < base, total / per_block(roots), 0.0)
        squares = []
        for j in range(N[g]):
            own = jnp.where((lane >= j * HB) & (lane < (j + 1) * HB), fore * fore, 0.0)
            own = jnp.sum(own, axis=1, keepdims=True)
            squares.append(jnp.sum(own, axis=0, keepdims=True))
        return fore, squares, roots

    def len1(g):
        return lambda d: remote(
            s3[g], r3b[g].at[q], e1s.at[g, d], e1r.at[g, d], plane(d)[1], x
        )

    def len2(g):
        return lambda d: remote(
            s4[g], r4b[g].at[y], e2s.at[g, d], e2r.at[g, d], along_y(d)[1], x
        )

    def lengths_start(g, squares):
        line = spread(squares)
        s3[g][...] = line
        each(NP, lambda d: len1(g)(d).start())
        r3b[g][q] = line

    def lengths_turn(g):
        each(NP, lambda d: len1(g)(d).wait_recv())
        line = r3b[g][0]
        for p in range(1, NP):
            line = line + r3b[g][p]
        s4[g][...] = line
        each(NY, lambda d: len2(g)(d).start())
        r4b[g][y] = line

    def lengths_finish(g):
        each(NY, lambda d: len2(g)(d).wait_recv())
        line = r4b[g][0]
        for p in range(1, NY):
            line = line + r4b[g][p]
        lengths = [jnp.sqrt(pick(line, j) / FT + EPS) for j in range(N[g])]
        sigmas = [pick(line, j) / lengths[j] / math.sqrt(FT * DT) for j in range(N[g])]
        return lengths, [gam[FIRST[g] + j] / sigmas[j] for j in range(N[g])]

    def left_out(g, fore, lengths):
        left = fore / per_block(lengths)
        keep = (diag >= 0) & (lax.rem(diag, 8) == 0)

        def unpack(j, carry):
            own = pltpu.roll(left, lax.rem(128 - j * HB, 128), 1)
            rows = jnp.zeros((8, H), F32)
            for rb in range(HB):
                rows = jnp.where(diag == 8 * rb, own[:, rb : rb + 1], rows)
            rows = jnp.where(keep, rows, 0.0)
            uout[pl.ds(FIRST[g] + j, 1), :] = jnp.sum(rows, axis=0, keepdims=True)
            return carry

        lax.fori_loop(0, N[g], unpack, 0)

    def right_out(g, roots):
        for j in range(N[g]):
            vout[FIRST[g] + j : FIRST[g] + j + 1, :] = bn[g][j : j + 1, :] / roots[j]

    swap = [
        remote(w16.at[pl.ds(pl.multiple_of(c * H, H), H)], w16.at[pl.ds(pl.multiple_of(c * H, H), H)],
               ks.at[0], kr.at[0], row + 1 - 2 * c, x),
        remote(w16.at[pl.ds(pl.multiple_of((2 + c) * H, H), H)], w16.at[pl.ds(pl.multiple_of((2 + c) * H, H), H)],
               ks.at[1], kr.at[1], row + 1 - 2 * c, x),
        remote(d16.at[pl.ds(pl.multiple_of(c * H, H), H)], d16.at[pl.ds(pl.multiple_of(c * H, H), H)],
               ks.at[2], kr.at[2], row + 1 - 2 * c, x),
    ]

    def tok_a1(d):
        return remote(tok_h.at[:, 0:W], ta.at[z], ta1s.at[d], ta1r.at[d], along_z(d)[1], x)

    def tok_b1(d):
        return remote(tok_h.at[:, W:D], tb.at[y], tb1s.at[d], tb1r.at[d], along_y(d)[1], x)

    def tok_a2(d):
        return remote(xa.at[y], xa.at[y], ta2s.at[d], ta2r.at[d], along_y(d)[1], x)

    def tok_b2(d):
        return remote(xb.at[z], xb.at[z], tb2s.at[d], tb2r.at[d], along_z(d)[1], x)

    def gates_out(d):
        return remote(
            gp.at[pl.ds(pl.multiple_of(along_x(d) * XT, XT), XT)], xr.at[x],
            gs.at[d], gr.at[d], row, along_x(d),
        )

    def gates_back(d):
        mine = ga.at[pl.ds(pl.multiple_of(x * XT, XT), XT)]
        return remote(mine, mine, hs.at[d], hr.at[d], row, along_x(d))

    def sum_a1(d, h):
        return remote(asrc.at[along_y(d)[0], h], adst.at[y, h], as1.at[h, d], ar1.at[h, d], along_y(d)[1], x)

    def sum_b1(d, h):
        return remote(bsrc.at[along_z(d)[0], h], bdst.at[z, h], bs1.at[h, d], br1.at[h, d], along_z(d)[1], x)

    def sum_a2(d):
        return remote(aq.at[along_z(d)[0]], ar.at[z], as2.at[d], ar2.at[d], along_z(d)[1], x)

    def sum_b2(d):
        return remote(bq.at[along_y(d)[0]], br.at[y], bs2.at[d], br2.at[d], along_y(d)[1], x)

    loads[0].wait()
    back_first(0)
    back_first(1)
    pl.semaphore_wait(barrier, (NP - 1) + (NY - 1) + (NX - 1))
    start1(0, 0)
    start1(1, 0)
    each(NZ, lambda d: tok_a1(d).start())
    each(NY, lambda d: tok_b1(d).start())
    w16[pl.ds(pl.multiple_of(c * H, H), H), :] = w[0].astype(BF16)
    w16[pl.ds(pl.multiple_of((2 + c) * H, H), H), :] = w[1].astype(BF16)
    d16[pl.ds(pl.multiple_of(c * H, H), H), :] = w[2].astype(BF16)
    start2(0, 0)
    start2(1, 0)

    loads[4].wait()
    each(NZ, lambda d: tok_a1(d).wait_recv())
    for p in range(NZ):
        tzf[T * p : T * p + T, :] = ta[p].astype(F32)
    xa[y] = tzf[...].astype(BF16)
    each(NY, lambda d: tok_a2(d).start())
    loads[5].wait()
    each(NY, lambda d: tok_b1(d).wait_recv())
    for p in range(NY):
        tzf[T * p : T * p + T, :] = tb[p].astype(F32)
    xb[z] = tzf[...].astype(BF16)
    lo = lax.broadcasted_iota(jnp.int32, (NY * ZT, NY * ZT), 0)
    hi = lax.broadcasted_iota(jnp.int32, (NY * ZT, NY * ZT), 1)
    major = jnp.zeros_like(lo)
    for p in range(1, NY):
        major = major + (lo >= p * ZT).astype(jnp.int32)
    minor = jnp.zeros_like(lo)
    for p in range(1, NZ):
        minor = minor + (lo - major * ZT >= p * T).astype(jnp.int32)
    wanted = minor * YT + major * T + (lo - major * ZT - minor * T)
    perm[...] = jnp.where(hi == wanted, 1.0, 0.0).astype(BF16)
    start3(0, 0)
    start3(1, 0)
    each(NZ, lambda d: tok_b2(d).start())
    finish3(0, 0)
    col_start(0, 0, fore_packed(0, bv[0].at[0]))
    finish3(1, 0)
    col_start(1, 0, fore_packed(1, bv[1].at[0]))
    for copy in swap:
        copy.start()
    fore, squares, _ = col_finish(0, 0)
    back_second(0, fore, squares)
    start1(0, 1)
    fore, squares, _ = col_finish(1, 0)
    back_second(1, fore, squares)
    start1(1, 1)

    each(NY, lambda d: tok_a2(d).wait_recv())
    for p in range(NY):
        xf[ZT * p : ZT * p + ZT, :] = xa[p].astype(F32)
    x16[:, 0:W] = xf[...].astype(BF16)
    each(NZ, lambda d: tok_b2(d).wait_recv())
    for p in range(NZ):
        xf[YT * p : YT * p + YT, :] = xb[p].astype(F32)
    x16[:, W:D] = jnp.dot(
        perm[...], xf[...].astype(BF16), preferred_element_type=F32
    ).astype(BF16)
    swap[0].wait_recv()
    swap[1].wait_recv()
    gp[...] = lax.dot_general(
        x16[...], w16[...], (((1,), (1,)), ((), ())), preferred_element_type=F32
    )
    each(NX, lambda d: gates_out(d).start())
    xr[x] = gp[pl.ds(pl.multiple_of(x * XT, XT), XT), :]

    start2(0, 1)
    start2(1, 1)
    start3(0, 1)
    start3(1, 1)
    each(NX, lambda d: gates_out(d).wait_recv())
    total = xr[0]
    for p in range(1, NX):
        total = total + xr[p]
    ga[pl.ds(pl.multiple_of(x * XT, XT), XT), :] = total
    finish3(0, 1)
    normalise(0)
    col_start(0, 1, fore_packed(0, bn[0]))
    finish3(1, 1)
    normalise(1)
    col_start(1, 1, fore_packed(1, bn[1]))
    each(NX, lambda d: gates_back(d).start())
    fore_0, squares, roots_0 = col_finish(0, 1)
    lengths_start(0, squares)
    fore_1, squares, roots_1 = col_finish(1, 1)
    lengths_start(1, squares)
    right_out(0, roots_0)
    right_out(1, roots_1)
    lengths_turn(0)
    swap[2].wait_recv()
    each(NX, lambda d: gates_back(d).wait_recv())
    loads[6].wait()
    lengths_0, scales_0 = lengths_finish(0)
    gate = ga[:, 0 : 2 * H] * scales_0[0]
    upper = ga[:, 2 * H : 4 * H]
    hid[...] = (gate * jax.nn.sigmoid(gate) * upper).astype(BF16)

    lengths_turn(1)
    turned = jnp.dot(perm[...], hid[...], preferred_element_type=F32).astype(BF16)
    for h in range(2):
        out = jnp.dot(hid[...], d16[:, h * Q : h * Q + Q], preferred_element_type=F32)
        for p in range(NY):
            asrc[p, h] = out[ZT * p : ZT * p + ZT].astype(BF16)
        each(NY, lambda d: sum_a1(d, h).start())
        out = jnp.dot(turned, d16[:, W + h * Q : W + h * Q + Q], preferred_element_type=F32)
        for p in range(NZ):
            bsrc[p, h] = out[YT * p : YT * p + YT].astype(BF16)
        each(NZ, lambda d: sum_b1(d, h).start())
    adst[y] = asrc[y]
    bdst[z] = bsrc[z]

    lengths_1, scales_1 = lengths_finish(1)
    left_out(0, fore_0, lengths_0)
    left_out(1, fore_1, lengths_1)

    for g in range(2):
        for t in range(2):
            each(NP, lambda d: leg1(g, t)(d).wait_send())
            each(NY, lambda d: leg2(g, t)(d).wait_send())
            each(NP, lambda d: leg3(g, t)(d).wait_send())
            each(NX, lambda d: cross(g, t)(d).wait_send())
        each(NP, lambda d: len1(g)(d).wait_send())
        each(NY, lambda d: len2(g)(d).wait_send())
    for copy in swap:
        copy.wait_send()
    each(NZ, lambda d: tok_a1(d).wait_send())
    each(NY, lambda d: tok_b1(d).wait_send())
    each(NY, lambda d: tok_a2(d).wait_send())
    each(NZ, lambda d: tok_b2(d).wait_send())
    each(NX, lambda d: gates_out(d).wait_send())
    each(NX, lambda d: gates_back(d).wait_send())

    for h in range(2):
        each(NY, lambda d: sum_a1(d, h).wait_recv())
        total = adst[0, h].astype(F32)
        for p in range(1, NY):
            total = total + adst[p, h].astype(F32)
        acc[:, h * Q : h * Q + Q] = total
        if h == 1:
            for p in range(NZ):
                aq[p] = acc[T * p : T * p + T, :].astype(BF16)
            each(NZ, lambda d: sum_a2(d).start())
            ar[z] = aq[z]
        each(NZ, lambda d: sum_b1(d, h).wait_recv())
        total = bdst[0, h].astype(F32)
        for p in range(1, NZ):
            total = total + bdst[p, h].astype(F32)
        acb[:, h * Q : h * Q + Q] = total
    for p in range(NY):
        bq[p] = acb[T * p : T * p + T, :].astype(BF16)
    each(NY, lambda d: sum_b2(d).start())
    br[y] = bq[y]
    for h in range(2):
        each(NY, lambda d: sum_a1(d, h).wait_send())
        each(NZ, lambda d: sum_b1(d, h).wait_send())
    each(NZ, lambda d: sum_a2(d).wait_recv())
    total = ar[0].astype(F32)
    for p in range(1, NZ):
        total = total + ar[p].astype(F32)
    mixed[:, 0:W] = (total * scales_1[0] * scales_1[1]).astype(BF16)
    each(NY, lambda d: sum_b2(d).wait_recv())
    total = br[0].astype(F32)
    for p in range(1, NY):
        total = total + br[p].astype(F32)
    mixed[:, W:D] = (total * scales_1[0] * scales_1[1]).astype(BF16)
    each(NZ, lambda d: sum_a2(d).wait_send())
    each(NY, lambda d: sum_b2(d).wait_send())


def hand_over(a, b, c, d, e, f, sems):
    copies = [
        pltpu.make_async_copy(source, target, sems.at[i])
        for i, (source, target) in enumerate(((a, d), (b, e), (c, f)))
    ]
    for copy in copies:
        copy.start()
    for copy in copies:
        copy.wait()


def solution(mesh):
    rows, NX = mesh.shape["row"], mesh.shape["col"]
    NZ = math.isqrt(rows // 2)
    NY = rows // 2 // NZ
    NP = 2 * NZ

    def per_device(tokens, gate_weight, up_weight, down_weight, u_init, gammas):
        T, D = tokens.shape
        H = gate_weight.shape[0]
        ZT = NZ * T
        NT = NY * ZT
        XT = NT // NX
        W = D // 2
        Q = W // 2
        YT = NY * T
        dims = (NX, NY, NZ, H, D, T, D * NX, H * rows)
        V = pltpu.VMEM
        dma = pltpu.SemaphoreType.DMA

        def group(rows, n):
            return [
                V((2, rows, D), F32), V((2, NP, rows, 128), F32), V((2, rows, 128), F32),
                V((2, NY, rows, 128), F32), V((2, rows, 128), F32), V((2, rows, D), F32), V((n, D), F32),
                V((2, 8, 128), F32), V((2, NX, 8, 128), F32),
                V((1, 128), F32), V((NP, 1, 128), F32), V((1, 128), F32), V((NY, 1, 128), F32),
            ]

        anywhere = pl.BlockSpec(memory_space=pl.ANY)
        vmem = pl.BlockSpec(memory_space=pltpu.VMEM)
        held = pl.pallas_call(
            functools.partial(kernel, dims),
            out_shape=(
                V((T, D), BF16),
                V((3, H), F32),
                V((3, D), F32),
            ),
            in_specs=[anywhere] * 6,
            out_specs=(vmem, vmem, vmem),
            scratch_shapes=[
                pltpu.SMEM((3,), F32),
                V((3, H, D), F32), V((4 * H, D), BF16), V((2 * H, D), BF16), V((3, H), F32),
                V((NZ, T, W), BF16), V((NY, T, W), BF16), V((ZT, W), F32),
                V((NY, ZT, W), BF16), V((NZ, YT, W), BF16), V((NT, W), F32), V((NT, D), BF16), V((NT, NT), BF16),
                *(ref for g in range(2) for ref in group((2, 4)[g], (1, 2)[g])),
                V((NT, 4 * H), F32), V((NX, XT, 4 * H), F32), V((NT, 4 * H), F32), V((NT, 2 * H), BF16),
                V((NY, 2, ZT, Q), BF16), V((NY, 2, ZT, Q), BF16), V((NZ, 2, YT, Q), BF16), V((NZ, 2, YT, Q), BF16),
                V((ZT, W), F32), V((YT, W), F32),
                V((NZ, T, W), BF16), V((NZ, T, W), BF16), V((NY, T, W), BF16), V((NY, T, W), BF16),
                dma((3,)), dma((4,)),
                dma((2, 2, NP)), dma((2, 2, NP)), dma((2, 2, NY)), dma((2, 2, NY)), dma((2, 2, NP)), dma((2, 2, NP)),
                dma((2, 2, NX)), dma((2, 2, NX)),
                dma((2, NP)), dma((2, NP)), dma((2, NY)), dma((2, NY)), dma((3,)), dma((3,)),
                dma((NZ,)), dma((NZ,)), dma((NY,)), dma((NY,)), dma((NY,)), dma((NY,)), dma((NZ,)), dma((NZ,)),
                dma((NX,)), dma((NX,)), dma((NX,)), dma((NX,)),
                dma((2, NY)), dma((2, NY)), dma((2, NZ)), dma((2, NZ)), dma((NZ,)), dma((NZ,)), dma((NY,)), dma((NY,)),
            ],
            compiler_params=pltpu.CompilerParams(
                collective_id=0, has_side_effects=True, vmem_limit_bytes=60 * 1024 * 1024
            ),
        )(tokens, gate_weight, up_weight, down_weight, u_init, gammas)
        return pl.pallas_call(
            hand_over,
            out_shape=tuple(jax.ShapeDtypeStruct(v.shape, v.dtype) for v in held),
            in_specs=[vmem] * 3,
            out_specs=(anywhere,) * 3,
            scratch_shapes=[dma((3,))],
            compiler_params=pltpu.CompilerParams(vmem_limit_bytes=1024 * 1024),
        )(*held)

    return jax.shard_map(
        per_device,
        mesh=mesh,
        in_specs=(
            P("row", "col"),
            P("row", "col"),
            P("row", "col"),
            P("row", "col"),
            P(None, "row"),
            P(),
        ),
        out_specs=(P("row", "col"), P(None, "row"), P(None, "col")),
        check_vma=False,
    )
```

```python
import functools
import math

import jax
import jax.numpy as jnp
from jax import lax
from jax.experimental import pallas as pl
from jax.experimental.pallas import tpu as pltpu
from jax.sharding import PartitionSpec as P

MESH = pl.DeviceIdType.MESH
EPS = 1e-06
F32 = jnp.float32
BF16 = jnp.bfloat16


def kernel(
    dims,
    tok_h, wg_h, wu_h, wd_h, ui_h, gam_h,
    mixed, uout, vout,
    gam, w, w16, d16, ui, ta, tb, tzf, xa, xb, xf, x16, perm,
    part_0, r1b_0, r1s_0, r2b_0, r2s_0, bv_0, bn_0, pk_0, cb_0, s3_0, r3b_0, s4_0, r4b_0,
    part_1, r1b_1, r1s_1, r2b_1, r2s_1, bv_1, bn_1, pk_1, cb_1, s3_1, r3b_1, s4_1, r4b_1,
    gp, xr, ga, hid, asrc, adst, apre, bsrc, bdst, bpre, acc, acb, aq, ar, bq, br,
    wsem, lsem, p1s, p1r, p2s, p2r, p3s, p3r, cs, cr,
    e1s, e1r, e2s, e2r, ks, kr, ta1s, ta1r, tb1s, tb1r, ta2s, ta2r, tb2s, tb2r,
    gs, gr, hs, hr, as1, ar1, ap1, aq1, bs1, br1, bp1, bq1, as2, ar2, bs2, br2,
):
    NX, NY, NZ, H, D, T, DT, FT = dims
    FIRST, N, ROWS = (0, 1), (1, 2), (2, 4)
    part, r1b, r1s, r2b, r2s = (part_0, part_1), (r1b_0, r1b_1), (r1s_0, r1s_1), (r2b_0, r2b_1), (r2s_0, r2s_1)
    bv, bn, pk, cb = (bv_0, bv_1), (bn_0, bn_1), (pk_0, pk_1), (cb_0, cb_1)
    s3, r3b, s4, r4b = (s3_0, s3_1), (r3b_0, r3b_1), (s4_0, s4_1), (r4b_0, r4b_1)
    NP = 2 * NZ
    HB = H // 8
    ZT = NZ * T
    YT = NY * T
    XT = NY * ZT // NX
    W = D // 2
    Q = W // 2
    row = lax.axis_index("row")
    x = lax.axis_index("col")
    y = row // NP
    q = row & (NP - 1)
    z = q // 2
    c = q & 1

    def remote(src, dst, ssem, rsem, r, cc):
        return pltpu.make_async_remote_copy(
            src_ref=src, dst_ref=dst, send_sem=ssem, recv_sem=rsem,
            device_id={"row": r, "col": cc}, device_id_type=MESH,
        )

    def each(n, fn):
        for d in sorted(range(1, n), key=lambda d: -min(d, n - d)):
            fn(d)

    def turn(at, d, n):
        return (at + d) & (n - 1)

    def plane(d):
        p = turn(q, d, NP)
        return p, y * NP + p

    def along_y(d):
        p = turn(y, d, NY)
        return p, p * NP + q

    def along_z(d):
        p = turn(z, d, NZ)
        return p, y * NP + p * 2 + c

    def along_x(d):
        return turn(x, d, NX)

    def lanes(p, n=128):
        return pl.ds(pl.multiple_of(p * n, n), n)

    barrier = pltpu.get_barrier_semaphore()

    def greet(r, cc):
        pl.semaphore_signal(
            barrier, inc=1, device_id={"row": r, "col": cc}, device_id_type=MESH
        )

    each(NY, lambda d: greet(along_y(d)[1], x))
    each(NP, lambda d: greet(plane(d)[1], x))
    each(NX, lambda d: greet(row, along_x(d)))

    loads = [
        pltpu.make_async_copy(ui_h, ui, lsem.at[0]),
        pltpu.make_async_copy(wg_h, w.at[0], wsem.at[0]),
        pltpu.make_async_copy(wu_h, w.at[1], wsem.at[1]),
        pltpu.make_async_copy(wd_h, w.at[2], wsem.at[2]),
        pltpu.make_async_copy(tok_h.at[:, 0:W], ta.at[z], lsem.at[1]),
        pltpu.make_async_copy(tok_h.at[:, W:D], tb.at[y], lsem.at[2]),
        pltpu.make_async_copy(gam_h, gam, lsem.at[3]),
    ]
    for load in loads:
        load.start()

    lane = lax.broadcasted_iota(jnp.int32, (8, 128), 1)
    lane1 = lax.broadcasted_iota(jnp.int32, (1, 128), 1)
    hl = lax.broadcasted_iota(jnp.int32, (8, H), 1)
    hs_ = lax.broadcasted_iota(jnp.int32, (8, H), 0)
    diag = hl - hs_

    def spread(values):
        out = jnp.zeros((1, 128), F32)
        for k, value in enumerate(values):
            out = jnp.where(lane1 == k, value, out)
        return out

    def per_block(values):
        out = values[-1]
        for k in reversed(range(len(values) - 1)):
            out = jnp.where(lane1 < (k + 1) * HB, values[k], out)
        return out

    def pick(vector, k):
        return vector[:, k : k + 1]

    def back_first(g):
        def body(j, carry):
            k = FIRST[g] + j
            pltpu.make_async_copy(w.at[k], w.at[k], wsem.at[k]).wait()
            left = jnp.broadcast_to(ui[pl.ds(k, 1), :], (8, H))
            total = jnp.zeros((8, D), F32)
            for rb in range(HB):
                col = jnp.sum(jnp.where(diag == 8 * rb, left, 0.0), axis=1, keepdims=True)
                total = total + w[k, 8 * rb : 8 * rb + 8, :] * col
            part[g][0, pl.ds(j, 1), :] = jnp.sum(total, axis=0, keepdims=True)
            return carry
        lax.fori_loop(0, N[g], body, 0)
        part[g][0, N[g] : ROWS[g], :] = jnp.zeros((ROWS[g] - N[g], D), F32)

    def back_second(g, fore, squares):
        def body(j, carry):
            left = pltpu.roll(fore, lax.rem(128 - j * HB, 128), 1)
            total = jnp.zeros((8, D), F32)
            for rb in range(HB):
                total = total + w[FIRST[g] + j, 8 * rb : 8 * rb + 8, :] * left[:, rb : rb + 1]
            part[g][1, pl.ds(j, 1), :] = jnp.sum(total, axis=0, keepdims=True)
            return carry
        lax.fori_loop(0, N[g], body, 0)
        line = jnp.broadcast_to(spread(squares), (ROWS[g] - N[g], 128))
        for p in range(NP):
            part[g][1, N[g] : ROWS[g], 128 * p : 128 * p + 128] = line

    def fore_packed(g, source):
        def body(j, packed):
            b = source[pl.ds(j, 1), :]
            b8 = jnp.broadcast_to(b, (8, D))
            mine = jnp.zeros((8, 128), F32)
            for rb in range(HB):
                got = jnp.sum(w[FIRST[g] + j, 8 * rb : 8 * rb + 8, :] * b8, axis=1, keepdims=True)
                mine = jnp.where(lane == rb, got, mine)
            packed = packed + pltpu.roll(mine, j * HB, 1)
            square = jnp.sum(b * b, axis=1, keepdims=True)
            return jnp.where(lane == N[g] * HB + j, square, packed)
        return lax.fori_loop(0, N[g], body, jnp.zeros((8, 128), F32))

    def leg1(g, t):
        return lambda d: remote(
            part[g].at[t, :, lanes(plane(d)[0])], r1b[g].at[t, q],
            p1s.at[g, t, d], p1r.at[g, t, d], plane(d)[1], x,
        )

    def leg2(g, t):
        return lambda d: remote(
            r1s[g].at[t], r2b[g].at[t, y], p2s.at[g, t, d], p2r.at[g, t, d], along_y(d)[1], x
        )

    def leg3(g, t):
        return lambda d: remote(
            r2s[g].at[t], bv[g].at[t, :, lanes(q)], p3s.at[g, t, d], p3r.at[g, t, d], plane(d)[1], x
        )

    def start1(g, t):
        each(NP, lambda d: leg1(g, t)(d).start())
        r1b[g][t, q] = part[g][t, :, lanes(q)]

    def start2(g, t):
        each(NP, lambda d: leg1(g, t)(d).wait_recv())
        total = r1b[g][t, 0]
        for p in range(1, NP):
            total = total + r1b[g][t, p]
        r1s[g][t] = total
        each(NY, lambda d: leg2(g, t)(d).start())
        r2b[g][t, y] = total

    def start3(g, t):
        each(NY, lambda d: leg2(g, t)(d).wait_recv())
        total = r2b[g][t, 0]
        for p in range(1, NY):
            total = total + r2b[g][t, p]
        r2s[g][t] = total
        each(NP, lambda d: leg3(g, t)(d).start())
        bv[g][t, :, lanes(q)] = total

    def finish3(g, t):
        each(NP, lambda d: leg3(g, t)(d).wait_recv())

    def normalise(g):
        line = bv[g][1, N[g] : N[g] + 1, 0:128]
        for j in range(N[g]):
            bn[g][j : j + 1, :] = bv[g][1, j : j + 1, :] / jnp.sqrt(pick(line, j) / FT + EPS)

    def cross(g, t):
        return lambda d: remote(
            pk[g].at[t], cb[g].at[t, x], cs.at[g, t, d], cr.at[g, t, d], row, along_x(d)
        )

    def col_start(g, t, packed):
        pk[g][t] = packed
        each(NX, lambda d: cross(g, t)(d).start())
        cb[g][t, x] = packed

    def col_finish(g, t):
        each(NX, lambda d: cross(g, t)(d).wait_recv())
        total = cb[g][t, 0]
        for p in range(1, NX):
            total = total + cb[g][t, p]
        base = N[g] * HB
        roots = [
            jnp.sqrt(total[0:1, base + j : base + j + 1] / DT + EPS) for j in range(N[g])
        ]
        fore = jnp.where(lane < base, total / per_block(roots), 0.0)
        squares = []
        for j in range(N[g]):
            own = jnp.where((lane >= j * HB) & (lane < (j + 1) * HB), fore * fore, 0.0)
            own = jnp.sum(own, axis=1, keepdims=True)
            squares.append(jnp.sum(own, axis=0, keepdims=True))
        return fore, squares, roots

    def len1(g):
        return lambda d: remote(
            s3[g], r3b[g].at[q], e1s.at[g, d], e1r.at[g, d], plane(d)[1], x
        )

    def len2(g):
        return lambda d: remote(
            s4[g], r4b[g].at[y], e2s.at[g, d], e2r.at[g, d], along_y(d)[1], x
        )

    def lengths_start(g, squares):
        line = spread(squares)
        s3[g][...] = line
        each(NP, lambda d: len1(g)(d).start())
        r3b[g][q] = line

    def lengths_turn(g):
        each(NP, lambda d: len1(g)(d).wait_recv())
        line = r3b[g][0]
        for p in range(1, NP):
            line = line + r3b[g][p]
        s4[g][...] = line
        each(NY, lambda d: len2(g)(d).start())
        r4b[g][y] = line

    def lengths_finish(g):
        each(NY, lambda d: len2(g)(d).wait_recv())
        line = r4b[g][0]
        for p in range(1, NY):
            line = line + r4b[g][p]
        lengths = [jnp.sqrt(pick(line, j) / FT + EPS) for j in range(N[g])]
        sigmas = [pick(line, j) / lengths[j] / math.sqrt(FT * DT) for j in range(N[g])]
        return lengths, [gam[FIRST[g] + j] / sigmas[j] for j in range(N[g])]

    def left_out(g, fore, lengths):
        left = fore / per_block(lengths)
        keep = (diag >= 0) & (lax.rem(diag, 8) == 0)

        def unpack(j, carry):
            own = pltpu.roll(left, lax.rem(128 - j * HB, 128), 1)
            rows = jnp.zeros((8, H), F32)
            for rb in range(HB):
                rows = jnp.where(diag == 8 * rb, own[:, rb : rb + 1], rows)
            rows = jnp.where(keep, rows, 0.0)
            uout[pl.ds(FIRST[g] + j, 1), :] = jnp.sum(rows, axis=0, keepdims=True)
            return carry

        lax.fori_loop(0, N[g], unpack, 0)

    def right_out(g, roots):
        for j in range(N[g]):
            vout[FIRST[g] + j : FIRST[g] + j + 1, :] = bn[g][j : j + 1, :] / roots[j]

    swap = [
        remote(w16.at[pl.ds(pl.multiple_of(c * H, H), H)], w16.at[pl.ds(pl.multiple_of(c * H, H), H)],
               ks.at[0], kr.at[0], row + 1 - 2 * c, x),
        remote(w16.at[pl.ds(pl.multiple_of((2 + c) * H, H), H)], w16.at[pl.ds(pl.multiple_of((2 + c) * H, H), H)],
               ks.at[1], kr.at[1], row + 1 - 2 * c, x),
        remote(d16.at[pl.ds(pl.multiple_of(c * H, H), H)], d16.at[pl.ds(pl.multiple_of(c * H, H), H)],
               ks.at[2], kr.at[2], row + 1 - 2 * c, x),
    ]

    def tok_a1(d):
        return remote(tok_h.at[:, 0:W], ta.at[z], ta1s.at[d], ta1r.at[d], along_z(d)[1], x)

    def tok_b1(d):
        return remote(tok_h.at[:, W:D], tb.at[y], tb1s.at[d], tb1r.at[d], along_y(d)[1], x)

    def tok_a2(d):
        return remote(xa.at[y], xa.at[y], ta2s.at[d], ta2r.at[d], along_y(d)[1], x)

    def tok_b2(d):
        return remote(xb.at[z], xb.at[z], tb2s.at[d], tb2r.at[d], along_z(d)[1], x)

    def gates_out(d):
        return remote(
            gp.at[pl.ds(pl.multiple_of(along_x(d) * XT, XT), XT)], xr.at[x],
            gs.at[d], gr.at[d], row, along_x(d),
        )

    def gates_back(d):
        mine = ga.at[pl.ds(pl.multiple_of(x * XT, XT), XT)]
        return remote(mine, mine, hs.at[d], hr.at[d], row, along_x(d))

    def sum_a1(d, h):
        return remote(asrc.at[along_y(d)[0], h], adst.at[d, h], as1.at[h, d], ar1.at[h, d], along_y(d)[1], x)

    def sum_b1(d, h):
        return remote(bsrc.at[along_z(d)[0], h], bdst.at[d, h], bs1.at[h, d], br1.at[h, d], along_z(d)[1], x)

    def pre_a1(h):
        d = (1, NY - 1)[h]
        return remote(asrc.at[along_y(NY // 2)[0], h], apre.at[h], ap1.at[h], aq1.at[h], along_y(d)[1], x)

    def pre_b1(h):
        d = (1, NZ - 1)[h]
        return remote(bsrc.at[along_z(NZ // 2)[0], h], bpre.at[h], bp1.at[h], bq1.at[h], along_z(d)[1], x)

    def joined(n, h):
        return (n // 2 - 1, n // 2 + 1)[h]

    def direct(n, h):
        near = [d for d in range(1, n) if d not in (n // 2, joined(n, h))]
        return sorted(near, key=lambda d: -min(d, n - d))

    def early(n):
        return [d for d in direct(n, 0) if d < n // 2 or d == n - 1]

    def late(n):
        return [d for d in direct(n, 0) if d not in early(n)]

    def join_a1(h):
        p = along_y(joined(NY, h))[0]
        pre_a1(h).wait_recv()
        asrc[p, h] = (asrc[p, h].astype(F32) + apre[h].astype(F32)).astype(BF16)
        sum_a1(joined(NY, h), h).start()

    def join_b1(h):
        p = along_z(joined(NZ, h))[0]
        pre_b1(h).wait_recv()
        bsrc[p, h] = (bsrc[p, h].astype(F32) + bpre[h].astype(F32)).astype(BF16)
        sum_b1(joined(NZ, h), h).start()

    def sum_a2(d):
        return remote(aq.at[along_z(d)[0]], ar.at[z], as2.at[d], ar2.at[d], along_z(d)[1], x)

    def sum_b2(d):
        return remote(bq.at[along_y(d)[0]], br.at[y], bs2.at[d], br2.at[d], along_y(d)[1], x)

    loads[0].wait()
    back_first(0)
    back_first(1)
    pl.semaphore_wait(barrier, (NP - 1) + (NY - 1) + (NX - 1))
    start1(0, 0)
    start1(1, 0)
    each(NZ, lambda d: tok_a1(d).start())
    each(NY, lambda d: tok_b1(d).start())
    w16[pl.ds(pl.multiple_of(c * H, H), H), :] = w[0].astype(BF16)
    w16[pl.ds(pl.multiple_of((2 + c) * H, H), H), :] = w[1].astype(BF16)
    d16[pl.ds(pl.multiple_of(c * H, H), H), :] = w[2].astype(BF16)
    start2(0, 0)
    start2(1, 0)

    loads[4].wait()
    each(NZ, lambda d: tok_a1(d).wait_recv())
    for p in range(NZ):
        tzf[T * p : T * p + T, :] = ta[p].astype(F32)
    xa[y] = tzf[...].astype(BF16)
    each(NY, lambda d: tok_a2(d).start())
    loads[5].wait()
    each(NY, lambda d: tok_b1(d).wait_recv())
    for p in range(NY):
        tzf[T * p : T * p + T, :] = tb[p].astype(F32)
    xb[z] = tzf[...].astype(BF16)
    lo = lax.broadcasted_iota(jnp.int32, (NY * ZT, NY * ZT), 0)
    hi = lax.broadcasted_iota(jnp.int32, (NY * ZT, NY * ZT), 1)
    major = jnp.zeros_like(lo)
    for p in range(1, NY):
        major = major + (lo >= p * ZT).astype(jnp.int32)
    minor = jnp.zeros_like(lo)
    for p in range(1, NZ):
        minor = minor + (lo - major * ZT >= p * T).astype(jnp.int32)
    wanted = minor * YT + major * T + (lo - major * ZT - minor * T)
    perm[...] = jnp.where(hi == wanted, 1.0, 0.0).astype(BF16)
    start3(0, 0)
    start3(1, 0)
    each(NZ, lambda d: tok_b2(d).start())
    finish3(0, 0)
    col_start(0, 0, fore_packed(0, bv[0].at[0]))
    finish3(1, 0)
    col_start(1, 0, fore_packed(1, bv[1].at[0]))
    for copy in swap:
        copy.start()
    fore, squares, _ = col_finish(0, 0)
    back_second(0, fore, squares)
    start1(0, 1)
    fore, squares, _ = col_finish(1, 0)
    back_second(1, fore, squares)
    start1(1, 1)

    each(NY, lambda d: tok_a2(d).wait_recv())
    for p in range(NY):
        xf[ZT * p : ZT * p + ZT, :] = xa[p].astype(F32)
    x16[:, 0:W] = xf[...].astype(BF16)
    each(NZ, lambda d: tok_b2(d).wait_recv())
    for p in range(NZ):
        xf[YT * p : YT * p + YT, :] = xb[p].astype(F32)
    x16[:, W:D] = jnp.dot(
        perm[...], xf[...].astype(BF16), preferred_element_type=F32
    ).astype(BF16)
    swap[0].wait_recv()
    swap[1].wait_recv()
    gp[...] = lax.dot_general(
        x16[...], w16[...], (((1,), (1,)), ((), ())), preferred_element_type=F32
    )
    each(NX, lambda d: gates_out(d).start())
    xr[x] = gp[pl.ds(pl.multiple_of(x * XT, XT), XT), :]

    start2(0, 1)
    start2(1, 1)
    start3(0, 1)
    start3(1, 1)
    each(NX, lambda d: gates_out(d).wait_recv())
    total = xr[0]
    for p in range(1, NX):
        total = total + xr[p]
    ga[pl.ds(pl.multiple_of(x * XT, XT), XT), :] = total
    finish3(0, 1)
    normalise(0)
    col_start(0, 1, fore_packed(0, bn[0]))
    finish3(1, 1)
    normalise(1)
    col_start(1, 1, fore_packed(1, bn[1]))
    each(NX, lambda d: gates_back(d).start())
    fore_0, squares, roots_0 = col_finish(0, 1)
    lengths_start(0, squares)
    fore_1, squares, roots_1 = col_finish(1, 1)
    lengths_start(1, squares)
    right_out(0, roots_0)
    right_out(1, roots_1)
    lengths_turn(0)
    swap[2].wait_recv()
    each(NX, lambda d: gates_back(d).wait_recv())
    loads[6].wait()
    lengths_0, scales_0 = lengths_finish(0)
    gate = ga[:, 0 : 2 * H] * scales_0[0]
    upper = ga[:, 2 * H : 4 * H]
    hid[...] = (gate * jax.nn.sigmoid(gate) * upper).astype(BF16)

    lengths_turn(1)
    turned = jnp.dot(perm[...], hid[...], preferred_element_type=F32).astype(BF16)
    for h in range(2):
        out = jnp.dot(hid[...], d16[:, h * Q : h * Q + Q], preferred_element_type=F32)
        for p in range(NY):
            asrc[p, h] = out[ZT * p : ZT * p + ZT].astype(BF16)
        pre_a1(h).start()
        for d in (early(NY), direct(NY, 1))[h]:
            sum_a1(d, h).start()
        if h == 1:
            for d in late(NY):
                sum_a1(d, 0).start()
        out = jnp.dot(turned, d16[:, W + h * Q : W + h * Q + Q], preferred_element_type=F32)
        for p in range(NZ):
            bsrc[p, h] = out[YT * p : YT * p + YT].astype(BF16)
        pre_b1(h).start()
        for d in (early(NZ), direct(NZ, 1))[h]:
            sum_b1(d, h).start()
        if h == 1:
            for d in late(NZ):
                sum_b1(d, 0).start()
    adst[0] = asrc[y]
    bdst[0] = bsrc[z]
    left_out(0, fore_0, lengths_0)
    for h in range(2):
        join_a1(h)
        join_b1(h)

    lengths_1, scales_1 = lengths_finish(1)
    left_out(1, fore_1, lengths_1)

    for g in range(2):
        for t in range(2):
            each(NP, lambda d: leg1(g, t)(d).wait_send())
            each(NY, lambda d: leg2(g, t)(d).wait_send())
            each(NP, lambda d: leg3(g, t)(d).wait_send())
            each(NX, lambda d: cross(g, t)(d).wait_send())
        each(NP, lambda d: len1(g)(d).wait_send())
        each(NY, lambda d: len2(g)(d).wait_send())
    for copy in swap:
        copy.wait_send()
    each(NZ, lambda d: tok_a1(d).wait_send())
    each(NY, lambda d: tok_b1(d).wait_send())
    each(NY, lambda d: tok_a2(d).wait_send())
    each(NZ, lambda d: tok_b2(d).wait_send())
    each(NX, lambda d: gates_out(d).wait_send())
    each(NX, lambda d: gates_back(d).wait_send())

    for h in range(2):
        total = adst[0, h].astype(F32)
        for d in direct(NY, h) + [joined(NY, h)]:
            sum_a1(d, h).wait_recv()
        for d in direct(NY, h) + [joined(NY, h)]:
            total = total + adst[d, h].astype(F32)
        acc[:, h * Q : h * Q + Q] = total
        if h == 1:
            for p in range(NZ):
                aq[p] = acc[T * p : T * p + T, :].astype(BF16)
            each(NZ, lambda d: sum_a2(d).start())
            ar[z] = aq[z]
        total = bdst[0, h].astype(F32)
        for d in direct(NZ, h) + [joined(NZ, h)]:
            sum_b1(d, h).wait_recv()
        for d in direct(NZ, h) + [joined(NZ, h)]:
            total = total + bdst[d, h].astype(F32)
        acb[:, h * Q : h * Q + Q] = total
    for p in range(NY):
        bq[p] = acb[T * p : T * p + T, :].astype(BF16)
    each(NY, lambda d: sum_b2(d).start())
    br[y] = bq[y]
    for h in range(2):
        pre_a1(h).wait_send()
        pre_b1(h).wait_send()
        for d in direct(NY, h) + [joined(NY, h)]:
            sum_a1(d, h).wait_send()
        for d in direct(NZ, h) + [joined(NZ, h)]:
            sum_b1(d, h).wait_send()
    each(NZ, lambda d: sum_a2(d).wait_recv())
    total = ar[0].astype(F32)
    for p in range(1, NZ):
        total = total + ar[p].astype(F32)
    mixed[:, 0:W] = (total * scales_1[0] * scales_1[1]).astype(BF16)
    each(NY, lambda d: sum_b2(d).wait_recv())
    total = br[0].astype(F32)
    for p in range(1, NY):
        total = total + br[p].astype(F32)
    mixed[:, W:D] = (total * scales_1[0] * scales_1[1]).astype(BF16)
    each(NZ, lambda d: sum_a2(d).wait_send())
    each(NY, lambda d: sum_b2(d).wait_send())


def hand_over(a, b, c, d, e, f, sems):
    copies = [
        pltpu.make_async_copy(source, target, sems.at[i])
        for i, (source, target) in enumerate(((a, d), (b, e), (c, f)))
    ]
    for copy in copies:
        copy.start()
    for copy in copies:
        copy.wait()


def solution(mesh):
    rows, NX = mesh.shape["row"], mesh.shape["col"]
    NZ = math.isqrt(rows // 2)
    NY = rows // 2 // NZ
    NP = 2 * NZ

    def per_device(tokens, gate_weight, up_weight, down_weight, u_init, gammas):
        T, D = tokens.shape
        H = gate_weight.shape[0]
        ZT = NZ * T
        NT = NY * ZT
        XT = NT // NX
        W = D // 2
        Q = W // 2
        YT = NY * T
        dims = (NX, NY, NZ, H, D, T, D * NX, H * rows)
        V = pltpu.VMEM
        dma = pltpu.SemaphoreType.DMA

        def group(rows, n):
            return [
                V((2, rows, D), F32), V((2, NP, rows, 128), F32), V((2, rows, 128), F32),
                V((2, NY, rows, 128), F32), V((2, rows, 128), F32), V((2, rows, D), F32), V((n, D), F32),
                V((2, 8, 128), F32), V((2, NX, 8, 128), F32),
                V((1, 128), F32), V((NP, 1, 128), F32), V((1, 128), F32), V((NY, 1, 128), F32),
            ]

        anywhere = pl.BlockSpec(memory_space=pl.ANY)
        vmem = pl.BlockSpec(memory_space=pltpu.VMEM)
        held = pl.pallas_call(
            functools.partial(kernel, dims),
            out_shape=(
                V((T, D), BF16),
                V((3, H), F32),
                V((3, D), F32),
            ),
            in_specs=[anywhere] * 6,
            out_specs=(vmem, vmem, vmem),
            scratch_shapes=[
                pltpu.SMEM((3,), F32),
                V((3, H, D), F32), V((4 * H, D), BF16), V((2 * H, D), BF16), V((3, H), F32),
                V((NZ, T, W), BF16), V((NY, T, W), BF16), V((ZT, W), F32),
                V((NY, ZT, W), BF16), V((NZ, YT, W), BF16), V((NT, W), F32), V((NT, D), BF16), V((NT, NT), BF16),
                *(ref for g in range(2) for ref in group((2, 4)[g], (1, 2)[g])),
                V((NT, 4 * H), F32), V((NX, XT, 4 * H), F32), V((NT, 4 * H), F32), V((NT, 2 * H), BF16),
                V((NY, 2, ZT, Q), BF16), V((NY, 2, ZT, Q), BF16), V((2, ZT, Q), BF16),
                V((NZ, 2, YT, Q), BF16), V((NZ, 2, YT, Q), BF16), V((2, YT, Q), BF16),
                V((ZT, W), F32), V((YT, W), F32),
                V((NZ, T, W), BF16), V((NZ, T, W), BF16), V((NY, T, W), BF16), V((NY, T, W), BF16),
                dma((3,)), dma((4,)),
                dma((2, 2, NP)), dma((2, 2, NP)), dma((2, 2, NY)), dma((2, 2, NY)), dma((2, 2, NP)), dma((2, 2, NP)),
                dma((2, 2, NX)), dma((2, 2, NX)),
                dma((2, NP)), dma((2, NP)), dma((2, NY)), dma((2, NY)), dma((3,)), dma((3,)),
                dma((NZ,)), dma((NZ,)), dma((NY,)), dma((NY,)), dma((NY,)), dma((NY,)), dma((NZ,)), dma((NZ,)),
                dma((NX,)), dma((NX,)), dma((NX,)), dma((NX,)),
                dma((2, NY)), dma((2, NY)), dma((2,)), dma((2,)), dma((2, NZ)), dma((2, NZ)), dma((2,)), dma((2,)),
                dma((NZ,)), dma((NZ,)), dma((NY,)), dma((NY,)),
            ],
            compiler_params=pltpu.CompilerParams(
                collective_id=0, has_side_effects=True, vmem_limit_bytes=60 * 1024 * 1024
            ),
        )(tokens, gate_weight, up_weight, down_weight, u_init, gammas)
        return pl.pallas_call(
            hand_over,
            out_shape=tuple(jax.ShapeDtypeStruct(v.shape, v.dtype) for v in held),
            in_specs=[vmem] * 3,
            out_specs=(anywhere,) * 3,
            scratch_shapes=[dma((3,))],
            compiler_params=pltpu.CompilerParams(vmem_limit_bytes=1024 * 1024),
        )(*held)

    return jax.shard_map(
        per_device,
        mesh=mesh,
        in_specs=(
            P("row", "col"),
            P("row", "col"),
            P("row", "col"),
            P("row", "col"),
            P(None, "row"),
            P(),
        ),
        out_specs=(P("row", "col"), P(None, "row"), P(None, "col")),
        check_vma=False,
    )
```

```python
import functools
import math

import jax
import jax.numpy as jnp
from jax import lax
from jax.experimental import pallas as pl
from jax.experimental.pallas import tpu as pltpu
from jax.sharding import PartitionSpec as P

MESH = pl.DeviceIdType.MESH
EPS = 1e-06
F32 = jnp.float32
BF16 = jnp.bfloat16


def kernel(
    dims,
    tok_h, wg_h, wu_h, wd_h, ui_h, gam_h,
    mixed, uout, vout,
    gam, w, w16, d16, ui, ta, tb, tzf, xa, xb, xf, x16, perm,
    part_0, r1b_0, r1s_0, r2b_0, r2s_0, bv_0, bn_0, pk_0, cb_0, s3_0, r3b_0, s4_0, r4b_0,
    part_1, r1b_1, r1s_1, r2b_1, r2s_1, bv_1, bn_1, pk_1, cb_1, s3_1, r3b_1, s4_1, r4b_1,
    gp, xr, ga, hid, asrc, adst, apre, bsrc, bdst, bpre, acc, acb, aq, ar, bq, br,
    wsem, lsem, p1s, p1r, p2s, p2r, p3s, p3r, cs, cr,
    e1s, e1r, e2s, e2r, ks, kr, ta1s, ta1r, tb1s, tb1r, ta2s, ta2r, tb2s, tb2r,
    gs, gr, hs, hr, as1, ar1, ap1, aq1, bs1, br1, bp1, bq1, as2, ar2, bs2, br2,
):
    NX, NY, NZ, H, D, T, DT, FT = dims
    FIRST, N, ROWS = (0, 1), (1, 2), (2, 4)
    part, r1b, r1s, r2b, r2s = (part_0, part_1), (r1b_0, r1b_1), (r1s_0, r1s_1), (r2b_0, r2b_1), (r2s_0, r2s_1)
    bv, bn, pk, cb = (bv_0, bv_1), (bn_0, bn_1), (pk_0, pk_1), (cb_0, cb_1)
    s3, r3b, s4, r4b = (s3_0, s3_1), (r3b_0, r3b_1), (s4_0, s4_1), (r4b_0, r4b_1)
    NP = 2 * NZ
    HB = H // 8
    ZT = NZ * T
    YT = NY * T
    XT = NY * ZT // NX
    W = D // 2
    Q = W // 2
    row = lax.axis_index("row")
    x = lax.axis_index("col")
    y = row // NP
    q = row & (NP - 1)
    z = q // 2
    c = q & 1

    def remote(src, dst, ssem, rsem, r, cc):
        return pltpu.make_async_remote_copy(
            src_ref=src, dst_ref=dst, send_sem=ssem, recv_sem=rsem,
            device_id={"row": r, "col": cc}, device_id_type=MESH,
        )

    def each(n, fn):
        for d in sorted(range(1, n), key=lambda d: -min(d, n - d)):
            fn(d)

    def turn(at, d, n):
        return (at + d) & (n - 1)

    def plane(d):
        p = turn(q, d, NP)
        return p, y * NP + p

    def along_y(d):
        p = turn(y, d, NY)
        return p, p * NP + q

    def along_z(d):
        p = turn(z, d, NZ)
        return p, y * NP + p * 2 + c

    def along_x(d):
        return turn(x, d, NX)

    def lanes(p, n=128):
        return pl.ds(pl.multiple_of(p * n, n), n)

    barrier = pltpu.get_barrier_semaphore()

    def greet(r, cc):
        pl.semaphore_signal(
            barrier, inc=1, device_id={"row": r, "col": cc}, device_id_type=MESH
        )

    each(NY, lambda d: greet(along_y(d)[1], x))
    each(NP, lambda d: greet(plane(d)[1], x))
    each(NX, lambda d: greet(row, along_x(d)))

    loads = [
        pltpu.make_async_copy(ui_h, ui, lsem.at[0]),
        pltpu.make_async_copy(wg_h, w.at[0], wsem.at[0]),
        pltpu.make_async_copy(wu_h, w.at[1], wsem.at[1]),
        pltpu.make_async_copy(wd_h, w.at[2], wsem.at[2]),
        pltpu.make_async_copy(tok_h.at[:, 0:W], ta.at[z], lsem.at[1]),
        pltpu.make_async_copy(tok_h.at[:, W:D], tb.at[y], lsem.at[2]),
        pltpu.make_async_copy(gam_h, gam, lsem.at[3]),
    ]
    for load in loads:
        load.start()

    lane = lax.broadcasted_iota(jnp.int32, (8, 128), 1)
    lane1 = lax.broadcasted_iota(jnp.int32, (1, 128), 1)
    hl = lax.broadcasted_iota(jnp.int32, (8, H), 1)
    hs_ = lax.broadcasted_iota(jnp.int32, (8, H), 0)
    diag = hl - hs_

    def spread(values):
        out = jnp.zeros((1, 128), F32)
        for k, value in enumerate(values):
            out = jnp.where(lane1 == k, value, out)
        return out

    def per_block(values):
        out = values[-1]
        for k in reversed(range(len(values) - 1)):
            out = jnp.where(lane1 < (k + 1) * HB, values[k], out)
        return out

    def pick(vector, k):
        return vector[:, k : k + 1]

    def back_first(g):
        def body(j, carry):
            k = FIRST[g] + j
            pltpu.make_async_copy(w.at[k], w.at[k], wsem.at[k]).wait()
            left = jnp.broadcast_to(ui[pl.ds(k, 1), :], (8, H))
            total = jnp.zeros((8, D), F32)
            for rb in range(HB):
                col = jnp.sum(jnp.where(diag == 8 * rb, left, 0.0), axis=1, keepdims=True)
                total = total + w[k, 8 * rb : 8 * rb + 8, :] * col
            part[g][0, pl.ds(j, 1), :] = jnp.sum(total, axis=0, keepdims=True)
            return carry
        lax.fori_loop(0, N[g], body, 0)
        part[g][0, N[g] : ROWS[g], :] = jnp.zeros((ROWS[g] - N[g], D), F32)

    def back_second(g, fore, squares):
        def body(j, carry):
            left = pltpu.roll(fore, lax.rem(128 - j * HB, 128), 1)
            total = jnp.zeros((8, D), F32)
            for rb in range(HB):
                total = total + w[FIRST[g] + j, 8 * rb : 8 * rb + 8, :] * left[:, rb : rb + 1]
            part[g][1, pl.ds(j, 1), :] = jnp.sum(total, axis=0, keepdims=True)
            return carry
        lax.fori_loop(0, N[g], body, 0)
        line = jnp.broadcast_to(spread(squares), (ROWS[g] - N[g], 128))
        for p in range(NP):
            part[g][1, N[g] : ROWS[g], 128 * p : 128 * p + 128] = line

    def fore_packed(g, source):
        def body(j, packed):
            b = source[pl.ds(j, 1), :]
            b8 = jnp.broadcast_to(b, (8, D))
            mine = jnp.zeros((8, 128), F32)
            for rb in range(HB):
                got = jnp.sum(w[FIRST[g] + j, 8 * rb : 8 * rb + 8, :] * b8, axis=1, keepdims=True)
                mine = jnp.where(lane == rb, got, mine)
            packed = packed + pltpu.roll(mine, j * HB, 1)
            square = jnp.sum(b * b, axis=1, keepdims=True)
            return jnp.where(lane == N[g] * HB + j, square, packed)
        return lax.fori_loop(0, N[g], body, jnp.zeros((8, 128), F32))

    def leg1(g, t):
        return lambda d: remote(
            part[g].at[t, :, lanes(plane(d)[0])], r1b[g].at[t, q],
            p1s.at[g, t, d], p1r.at[g, t, d], plane(d)[1], x,
        )

    def leg2(g, t):
        return lambda d: remote(
            r1s[g].at[t], r2b[g].at[t, y], p2s.at[g, t, d], p2r.at[g, t, d], along_y(d)[1], x
        )

    def leg3(g, t):
        return lambda d: remote(
            r2s[g].at[t], bv[g].at[t, :, lanes(q)], p3s.at[g, t, d], p3r.at[g, t, d], plane(d)[1], x
        )

    def start1(g, t):
        each(NP, lambda d: leg1(g, t)(d).start())
        r1b[g][t, q] = part[g][t, :, lanes(q)]

    def start2(g, t):
        each(NP, lambda d: leg1(g, t)(d).wait_recv())
        total = r1b[g][t, 0]
        for p in range(1, NP):
            total = total + r1b[g][t, p]
        r1s[g][t] = total
        each(NY, lambda d: leg2(g, t)(d).start())
        r2b[g][t, y] = total

    def start3(g, t):
        each(NY, lambda d: leg2(g, t)(d).wait_recv())
        total = r2b[g][t, 0]
        for p in range(1, NY):
            total = total + r2b[g][t, p]
        r2s[g][t] = total
        each(NP, lambda d: leg3(g, t)(d).start())
        bv[g][t, :, lanes(q)] = total

    def finish3(g, t):
        each(NP, lambda d: leg3(g, t)(d).wait_recv())

    def normalise(g):
        line = bv[g][1, N[g] : N[g] + 1, 0:128]
        for j in range(N[g]):
            bn[g][j : j + 1, :] = bv[g][1, j : j + 1, :] / jnp.sqrt(pick(line, j) / FT + EPS)

    def cross(g, t):
        return lambda d: remote(
            pk[g].at[t], cb[g].at[t, x], cs.at[g, t, d], cr.at[g, t, d], row, along_x(d)
        )

    def col_start(g, t, packed):
        pk[g][t] = packed
        each(NX, lambda d: cross(g, t)(d).start())
        cb[g][t, x] = packed

    def col_finish(g, t):
        each(NX, lambda d: cross(g, t)(d).wait_recv())
        total = cb[g][t, 0]
        for p in range(1, NX):
            total = total + cb[g][t, p]
        base = N[g] * HB
        roots = [
            jnp.sqrt(total[0:1, base + j : base + j + 1] / DT + EPS) for j in range(N[g])
        ]
        fore = jnp.where(lane < base, total / per_block(roots), 0.0)
        squares = []
        for j in range(N[g]):
            own = jnp.where((lane >= j * HB) & (lane < (j + 1) * HB), fore * fore, 0.0)
            own = jnp.sum(own, axis=1, keepdims=True)
            squares.append(jnp.sum(own, axis=0, keepdims=True))
        return fore, squares, roots

    def len1(g):
        return lambda d: remote(
            s3[g], r3b[g].at[q], e1s.at[g, d], e1r.at[g, d], plane(d)[1], x
        )

    def len2(g):
        return lambda d: remote(
            s4[g], r4b[g].at[y], e2s.at[g, d], e2r.at[g, d], along_y(d)[1], x
        )

    def lengths_start(g, squares):
        line = spread(squares)
        s3[g][...] = line
        each(NP, lambda d: len1(g)(d).start())
        r3b[g][q] = line

    def lengths_turn(g):
        each(NP, lambda d: len1(g)(d).wait_recv())
        line = r3b[g][0]
        for p in range(1, NP):
            line = line + r3b[g][p]
        s4[g][...] = line
        each(NY, lambda d: len2(g)(d).start())
        r4b[g][y] = line

    def lengths_finish(g):
        each(NY, lambda d: len2(g)(d).wait_recv())
        line = r4b[g][0]
        for p in range(1, NY):
            line = line + r4b[g][p]
        lengths = [jnp.sqrt(pick(line, j) / FT + EPS) for j in range(N[g])]
        sigmas = [pick(line, j) / lengths[j] / math.sqrt(FT * DT) for j in range(N[g])]
        return lengths, [gam[FIRST[g] + j] / sigmas[j] for j in range(N[g])]

    def left_out(g, fore, lengths):
        left = fore / per_block(lengths)
        keep = (diag >= 0) & (lax.rem(diag, 8) == 0)

        def unpack(j, carry):
            own = pltpu.roll(left, lax.rem(128 - j * HB, 128), 1)
            rows = jnp.zeros((8, H), F32)
            for rb in range(HB):
                rows = jnp.where(diag == 8 * rb, own[:, rb : rb + 1], rows)
            rows = jnp.where(keep, rows, 0.0)
            uout[pl.ds(FIRST[g] + j, 1), :] = jnp.sum(rows, axis=0, keepdims=True)
            return carry

        lax.fori_loop(0, N[g], unpack, 0)

    def right_out(g, roots):
        for j in range(N[g]):
            vout[FIRST[g] + j : FIRST[g] + j + 1, :] = bn[g][j : j + 1, :] / roots[j]

    swap = [
        remote(w16.at[pl.ds(pl.multiple_of(c * H, H), H)], w16.at[pl.ds(pl.multiple_of(c * H, H), H)],
               ks.at[0], kr.at[0], row + 1 - 2 * c, x),
        remote(w16.at[pl.ds(pl.multiple_of((2 + c) * H, H), H)], w16.at[pl.ds(pl.multiple_of((2 + c) * H, H), H)],
               ks.at[1], kr.at[1], row + 1 - 2 * c, x),
        remote(d16.at[pl.ds(pl.multiple_of(c * H, H), H)], d16.at[pl.ds(pl.multiple_of(c * H, H), H)],
               ks.at[2], kr.at[2], row + 1 - 2 * c, x),
    ]

    def tok_a1(d):
        return remote(tok_h.at[:, 0:W], ta.at[z], ta1s.at[d], ta1r.at[d], along_z(d)[1], x)

    def tok_b1(d):
        return remote(tok_h.at[:, W:D], tb.at[y], tb1s.at[d], tb1r.at[d], along_y(d)[1], x)

    def tok_a2(d):
        return remote(xa.at[y], xa.at[y], ta2s.at[d], ta2r.at[d], along_y(d)[1], x)

    def tok_b2(d):
        return remote(xb.at[z], xb.at[z], tb2s.at[d], tb2r.at[d], along_z(d)[1], x)

    def gates_out(d):
        return remote(
            gp.at[pl.ds(pl.multiple_of(along_x(d) * XT, XT), XT)], xr.at[x],
            gs.at[d], gr.at[d], row, along_x(d),
        )

    def gates_back(d):
        mine = ga.at[pl.ds(pl.multiple_of(x * XT, XT), XT)]
        return remote(mine, mine, hs.at[d], hr.at[d], row, along_x(d))

    def sum_a1(d, h):
        return remote(asrc.at[along_y(d)[0], h], adst.at[d, h], as1.at[h, d], ar1.at[h, d], along_y(d)[1], x)

    def sum_b1(d, h):
        return remote(bsrc.at[along_z(d)[0], h], bdst.at[d, h], bs1.at[h, d], br1.at[h, d], along_z(d)[1], x)

    def pre_a1(h):
        d = (1, NY - 1)[h]
        return remote(asrc.at[along_y(NY // 2)[0], h], apre.at[h], ap1.at[h], aq1.at[h], along_y(d)[1], x)

    def pre_b1(h):
        d = (1, NZ - 1)[h]
        return remote(bsrc.at[along_z(NZ // 2)[0], h], bpre.at[h], bp1.at[h], bq1.at[h], along_z(d)[1], x)

    def joined(n, h):
        return (n // 2 - 1, n // 2 + 1)[h]

    def direct(n, h):
        near = [d for d in range(1, n) if d not in (n // 2, joined(n, h))]
        return sorted(near, key=lambda d: -min(d, n - d))

    def early(n):
        return [d for d in direct(n, 0) if d < n // 2 or d == n - 1]

    def late(n):
        return [d for d in direct(n, 0) if d not in early(n)]

    def join_a1(h):
        p = along_y(joined(NY, h))[0]
        pre_a1(h).wait_recv()
        asrc[p, h] = (asrc[p, h].astype(F32) + apre[h].astype(F32)).astype(BF16)
        sum_a1(joined(NY, h), h).start()

    def join_b1(h):
        p = along_z(joined(NZ, h))[0]
        pre_b1(h).wait_recv()
        bsrc[p, h] = (bsrc[p, h].astype(F32) + bpre[h].astype(F32)).astype(BF16)
        sum_b1(joined(NZ, h), h).start()

    def sum_a2(d):
        return remote(aq.at[along_z(d)[0]], ar.at[z], as2.at[d], ar2.at[d], along_z(d)[1], x)

    def sum_b2(d):
        return remote(bq.at[along_y(d)[0]], br.at[y], bs2.at[d], br2.at[d], along_y(d)[1], x)

    loads[0].wait()
    back_first(0)
    back_first(1)
    pl.semaphore_wait(barrier, (NP - 1) + (NY - 1) + (NX - 1))
    start1(0, 0)
    start1(1, 0)
    each(NZ, lambda d: tok_a1(d).start())
    each(NY, lambda d: tok_b1(d).start())
    w16[pl.ds(pl.multiple_of(c * H, H), H), :] = w[0].astype(BF16)
    w16[pl.ds(pl.multiple_of((2 + c) * H, H), H), :] = w[1].astype(BF16)
    d16[pl.ds(pl.multiple_of(c * H, H), H), :] = w[2].astype(BF16)
    start2(0, 0)
    start2(1, 0)

    loads[4].wait()
    each(NZ, lambda d: tok_a1(d).wait_recv())
    for p in range(NZ):
        tzf[T * p : T * p + T, :] = ta[p].astype(F32)
    xa[y] = tzf[...].astype(BF16)
    loads[5].wait()
    each(NY, lambda d: tok_b1(d).wait_recv())
    for p in range(NY):
        tzf[T * p : T * p + T, :] = tb[p].astype(F32)
    xb[z] = tzf[...].astype(BF16)
    lo = lax.broadcasted_iota(jnp.int32, (NY * ZT, NY * ZT), 0)
    hi = lax.broadcasted_iota(jnp.int32, (NY * ZT, NY * ZT), 1)
    major = jnp.zeros_like(lo)
    for p in range(1, NY):
        major = major + (lo >= p * ZT).astype(jnp.int32)
    minor = jnp.zeros_like(lo)
    for p in range(1, NZ):
        minor = minor + (lo - major * ZT >= p * T).astype(jnp.int32)
    wanted = minor * YT + major * T + (lo - major * ZT - minor * T)
    perm[...] = jnp.where(hi == wanted, 1.0, 0.0).astype(BF16)
    start3(0, 0)
    start3(1, 0)
    each(NY, lambda d: tok_a2(d).start())
    each(NZ, lambda d: tok_b2(d).start())
    finish3(0, 0)
    col_start(0, 0, fore_packed(0, bv[0].at[0]))
    finish3(1, 0)
    col_start(1, 0, fore_packed(1, bv[1].at[0]))
    for copy in swap:
        copy.start()
    fore, squares, _ = col_finish(0, 0)
    back_second(0, fore, squares)
    start1(0, 1)
    fore, squares, _ = col_finish(1, 0)
    back_second(1, fore, squares)
    start1(1, 1)

    each(NY, lambda d: tok_a2(d).wait_recv())
    for p in range(NY):
        xf[ZT * p : ZT * p + ZT, :] = xa[p].astype(F32)
    x16[:, 0:W] = xf[...].astype(BF16)
    each(NZ, lambda d: tok_b2(d).wait_recv())
    for p in range(NZ):
        xf[YT * p : YT * p + YT, :] = xb[p].astype(F32)
    x16[:, W:D] = jnp.dot(
        perm[...], xf[...].astype(BF16), preferred_element_type=F32
    ).astype(BF16)
    swap[0].wait_recv()
    swap[1].wait_recv()
    gp[...] = lax.dot_general(
        x16[...], w16[...], (((1,), (1,)), ((), ())), preferred_element_type=F32
    )
    each(NX, lambda d: gates_out(d).start())
    xr[x] = gp[pl.ds(pl.multiple_of(x * XT, XT), XT), :]

    start2(0, 1)
    start2(1, 1)
    start3(0, 1)
    start3(1, 1)
    each(NX, lambda d: gates_out(d).wait_recv())
    total = xr[0]
    for p in range(1, NX):
        total = total + xr[p]
    ga[pl.ds(pl.multiple_of(x * XT, XT), XT), :] = total
    finish3(0, 1)
    normalise(0)
    col_start(0, 1, fore_packed(0, bn[0]))
    finish3(1, 1)
    normalise(1)
    col_start(1, 1, fore_packed(1, bn[1]))
    each(NX, lambda d: gates_back(d).start())
    fore_0, squares, roots_0 = col_finish(0, 1)
    lengths_start(0, squares)
    fore_1, squares, roots_1 = col_finish(1, 1)
    lengths_start(1, squares)
    right_out(0, roots_0)
    right_out(1, roots_1)
    lengths_turn(0)
    swap[2].wait_recv()
    each(NX, lambda d: gates_back(d).wait_recv())
    loads[6].wait()
    lengths_0, scales_0 = lengths_finish(0)
    gate = ga[:, 0 : 2 * H] * scales_0[0]
    upper = ga[:, 2 * H : 4 * H]
    hid[...] = (gate * jax.nn.sigmoid(gate) * upper).astype(BF16)

    lengths_turn(1)
    turned = jnp.dot(perm[...], hid[...], preferred_element_type=F32).astype(BF16)
    for h in range(2):
        out = jnp.dot(hid[...], d16[:, h * Q : h * Q + Q], preferred_element_type=F32)
        for p in range(NY):
            asrc[p, h] = out[ZT * p : ZT * p + ZT].astype(BF16)
        pre_a1(h).start()
        for d in (early(NY), direct(NY, 1))[h]:
            sum_a1(d, h).start()
        if h == 1:
            for d in late(NY):
                sum_a1(d, 0).start()
        out = jnp.dot(turned, d16[:, W + h * Q : W + h * Q + Q], preferred_element_type=F32)
        for p in range(NZ):
            bsrc[p, h] = out[YT * p : YT * p + YT].astype(BF16)
        pre_b1(h).start()
        for d in (early(NZ), direct(NZ, 1))[h]:
            sum_b1(d, h).start()
        if h == 1:
            for d in late(NZ):
                sum_b1(d, 0).start()
    adst[0] = asrc[y]
    bdst[0] = bsrc[z]
    left_out(0, fore_0, lengths_0)
    for h in range(2):
        join_a1(h)
        join_b1(h)

    lengths_1, scales_1 = lengths_finish(1)
    left_out(1, fore_1, lengths_1)

    for g in range(2):
        for t in range(2):
            each(NP, lambda d: leg1(g, t)(d).wait_send())
            each(NY, lambda d: leg2(g, t)(d).wait_send())
            each(NP, lambda d: leg3(g, t)(d).wait_send())
            each(NX, lambda d: cross(g, t)(d).wait_send())
        each(NP, lambda d: len1(g)(d).wait_send())
        each(NY, lambda d: len2(g)(d).wait_send())
    for copy in swap:
        copy.wait_send()
    each(NZ, lambda d: tok_a1(d).wait_send())
    each(NY, lambda d: tok_b1(d).wait_send())
    each(NY, lambda d: tok_a2(d).wait_send())
    each(NZ, lambda d: tok_b2(d).wait_send())
    each(NX, lambda d: gates_out(d).wait_send())
    each(NX, lambda d: gates_back(d).wait_send())

    for h in range(2):
        total = adst[0, h].astype(F32)
        for d in direct(NY, h) + [joined(NY, h)]:
            sum_a1(d, h).wait_recv()
        for d in direct(NY, h) + [joined(NY, h)]:
            total = total + adst[d, h].astype(F32)
        acc[:, h * Q : h * Q + Q] = total
        if h == 1:
            for p in range(NZ):
                aq[p] = acc[T * p : T * p + T, :].astype(BF16)
            each(NZ, lambda d: sum_a2(d).start())
            ar[z] = aq[z]
        total = bdst[0, h].astype(F32)
        for d in direct(NZ, h) + [joined(NZ, h)]:
            sum_b1(d, h).wait_recv()
        for d in direct(NZ, h) + [joined(NZ, h)]:
            total = total + bdst[d, h].astype(F32)
        acb[:, h * Q : h * Q + Q] = total
    for p in range(NY):
        bq[p] = acb[T * p : T * p + T, :].astype(BF16)
    each(NY, lambda d: sum_b2(d).start())
    br[y] = bq[y]
    for h in range(2):
        pre_a1(h).wait_send()
        pre_b1(h).wait_send()
        for d in direct(NY, h) + [joined(NY, h)]:
            sum_a1(d, h).wait_send()
        for d in direct(NZ, h) + [joined(NZ, h)]:
            sum_b1(d, h).wait_send()
    each(NZ, lambda d: sum_a2(d).wait_recv())
    total = ar[0].astype(F32)
    for p in range(1, NZ):
        total = total + ar[p].astype(F32)
    mixed[:, 0:W] = (total * scales_1[0] * scales_1[1]).astype(BF16)
    each(NY, lambda d: sum_b2(d).wait_recv())
    total = br[0].astype(F32)
    for p in range(1, NY):
        total = total + br[p].astype(F32)
    mixed[:, W:D] = (total * scales_1[0] * scales_1[1]).astype(BF16)
    each(NZ, lambda d: sum_a2(d).wait_send())
    each(NY, lambda d: sum_b2(d).wait_send())


def hand_over(a, b, c, d, e, f, sems):
    copies = [
        pltpu.make_async_copy(source, target, sems.at[i])
        for i, (source, target) in enumerate(((a, d), (b, e), (c, f)))
    ]
    for copy in copies:
        copy.start()
    for copy in copies:
        copy.wait()


def solution(mesh):
    rows, NX = mesh.shape["row"], mesh.shape["col"]
    NZ = math.isqrt(rows // 2)
    NY = rows // 2 // NZ
    NP = 2 * NZ

    def per_device(tokens, gate_weight, up_weight, down_weight, u_init, gammas):
        T, D = tokens.shape
        H = gate_weight.shape[0]
        ZT = NZ * T
        NT = NY * ZT
        XT = NT // NX
        W = D // 2
        Q = W // 2
        YT = NY * T
        dims = (NX, NY, NZ, H, D, T, D * NX, H * rows)
        V = pltpu.VMEM
        dma = pltpu.SemaphoreType.DMA

        def group(rows, n):
            return [
                V((2, rows, D), F32), V((2, NP, rows, 128), F32), V((2, rows, 128), F32),
                V((2, NY, rows, 128), F32), V((2, rows, 128), F32), V((2, rows, D), F32), V((n, D), F32),
                V((2, 8, 128), F32), V((2, NX, 8, 128), F32),
                V((1, 128), F32), V((NP, 1, 128), F32), V((1, 128), F32), V((NY, 1, 128), F32),
            ]

        anywhere = pl.BlockSpec(memory_space=pl.ANY)
        vmem = pl.BlockSpec(memory_space=pltpu.VMEM)
        held = pl.pallas_call(
            functools.partial(kernel, dims),
            out_shape=(
                V((T, D), BF16),
                V((3, H), F32),
                V((3, D), F32),
            ),
            in_specs=[anywhere] * 6,
            out_specs=(vmem, vmem, vmem),
            scratch_shapes=[
                pltpu.SMEM((3,), F32),
                V((3, H, D), F32), V((4 * H, D), BF16), V((2 * H, D), BF16), V((3, H), F32),
                V((NZ, T, W), BF16), V((NY, T, W), BF16), V((ZT, W), F32),
                V((NY, ZT, W), BF16), V((NZ, YT, W), BF16), V((NT, W), F32), V((NT, D), BF16), V((NT, NT), BF16),
                *(ref for g in range(2) for ref in group((2, 4)[g], (1, 2)[g])),
                V((NT, 4 * H), F32), V((NX, XT, 4 * H), F32), V((NT, 4 * H), F32), V((NT, 2 * H), BF16),
                V((NY, 2, ZT, Q), BF16), V((NY, 2, ZT, Q), BF16), V((2, ZT, Q), BF16),
                V((NZ, 2, YT, Q), BF16), V((NZ, 2, YT, Q), BF16), V((2, YT, Q), BF16),
                V((ZT, W), F32), V((YT, W), F32),
                V((NZ, T, W), BF16), V((NZ, T, W), BF16), V((NY, T, W), BF16), V((NY, T, W), BF16),
                dma((3,)), dma((4,)),
                dma((2, 2, NP)), dma((2, 2, NP)), dma((2, 2, NY)), dma((2, 2, NY)), dma((2, 2, NP)), dma((2, 2, NP)),
                dma((2, 2, NX)), dma((2, 2, NX)),
                dma((2, NP)), dma((2, NP)), dma((2, NY)), dma((2, NY)), dma((3,)), dma((3,)),
                dma((NZ,)), dma((NZ,)), dma((NY,)), dma((NY,)), dma((NY,)), dma((NY,)), dma((NZ,)), dma((NZ,)),
                dma((NX,)), dma((NX,)), dma((NX,)), dma((NX,)),
                dma((2, NY)), dma((2, NY)), dma((2,)), dma((2,)), dma((2, NZ)), dma((2, NZ)), dma((2,)), dma((2,)),
                dma((NZ,)), dma((NZ,)), dma((NY,)), dma((NY,)),
            ],
            compiler_params=pltpu.CompilerParams(
                collective_id=0, has_side_effects=True, vmem_limit_bytes=60 * 1024 * 1024
            ),
        )(tokens, gate_weight, up_weight, down_weight, u_init, gammas)
        return pl.pallas_call(
            hand_over,
            out_shape=tuple(jax.ShapeDtypeStruct(v.shape, v.dtype) for v in held),
            in_specs=[vmem] * 3,
            out_specs=(anywhere,) * 3,
            scratch_shapes=[dma((3,))],
            compiler_params=pltpu.CompilerParams(vmem_limit_bytes=1024 * 1024),
        )(*held)

    return jax.shard_map(
        per_device,
        mesh=mesh,
        in_specs=(
            P("row", "col"),
            P("row", "col"),
            P("row", "col"),
            P("row", "col"),
            P(None, "row"),
            P(),
        ),
        out_specs=(P("row", "col"), P(None, "row"), P(None, "col")),
        check_vma=False,
    )
```
